32 devices in a mesh: grp: 4 (over y, x), slab: 8 (over z, core).
Axes of the slice: x: 2, y: 2, z: 4, core: 2. Of those that a mesh axis runs over, the one named last changes fastest.
Arguments:
- forcing: float32 [4, 3, 64, 128, 128], P('grp', None, 'slab'), may hold values from -18 to 18
- stiffness: float32 [4, 3, 64, 128, 128], P('grp', None, 'slab'), may hold values from 0.25 to 4
- anisotropy: float32 [4, 3, 3], P('grp'), may hold values from 0.3 to 3
- coupling: float32 [4, 3, 3], P('grp'), may hold values from -0.3 to 2, as said below
- levels: int32 [4, 2], replicated, may hold values from 0 to 2
- neighbours: int32 [4, 3], replicated, may hold values from -1 to 3, as said below
Outputs:
- mixed: float32 [4, 3, 64, 128, 128], P('grp', None, 'slab')
The draws below stay inside these ranges and needn't reach their ends.
Inputs may be any that keep to these rules, and one draw needn't show every extreme that they name: neighbours[g, 0], [g, 1], [g, 2] name a pair whose levels are those of pair g less (1, 0), (0, 1), (1, 1), or are -1 where no pair has those levels. `coupling`: symmetric; diagonal entries 0.8 to 2, off-diagonal entries at most 0.3 in magnitude.
All inputs are finite; a program needn't handle non-finite values.
Results may differ from the reference program's by a relative error of at most 0.0003.
Values sent between devices are 32-bit elements; how exact they have to be, the bound alone decides.
No kernel may reach another device: no remote copies, remote signals or barrier semaphores. Data moves between devices by JAX's collectives and lax.ppermute only.
A program may use at most 64 MiB of HBM per device.

```python
import math
import jax
import jax.numpy as jnp
from jax import lax

ZD = 8
XMAX = 128
Y = 128
ITERS = 2
PAIRS = 4
ZMAX = 64
N_SLAB = 8


def index_table(key):
    base_key = jax.random.fold_in(key, 5)
    level_key, top_key, order_key, score_key = jax.random.split(base_key, 4)
    loose = jax.random.randint(level_key, (PAIRS, 2), 0, 3, dtype=jnp.int32)
    blocks = PAIRS // 4 + 1
    tops = jax.random.randint(top_key, (blocks, 2), 1, 3, dtype=jnp.int32)
    block_rows = jnp.arange(blocks, dtype=jnp.int32)[:, None]
    tops = jnp.where(block_rows == 0, 2, tops).astype(jnp.int32)
    member = jnp.arange(PAIRS, dtype=jnp.int32)
    block_of = member // 4
    role = member % 4
    lowering = jnp.array([[0, 0], [1, 0], [0, 1], [1, 1]], dtype=jnp.int32)
    grouped = jnp.take(tops, block_of, axis=0) - jnp.take(lowering, role, axis=0)
    in_block = (block_of < PAIRS // 4)[:, None]
    ordered = jnp.where(in_block, grouped, loose).astype(jnp.int32)
    ordered = jnp.where((member == PAIRS - 1)[:, None], 0, ordered).astype(jnp.int32)
    order = jax.random.permutation(order_key, PAIRS).astype(jnp.int32)
    levels = jnp.take(ordered, order, axis=0).astype(jnp.int32)
    offsets = jnp.array([[1, 0], [0, 1], [1, 1]], dtype=jnp.int32)
    wanted = levels[:, None, :] - offsets[None]
    matching = jnp.all(levels[None, None, :, :] == wanted[:, :, None, :], axis=-1)
    scores = jax.random.randint(score_key, (PAIRS, 3, PAIRS), 0, 65536, dtype=jnp.int32) * PAIRS
    scores = scores + jnp.arange(PAIRS, dtype=jnp.int32)[None, None, :]
    scores = jnp.where(matching, scores, -1)
    chosen = lax.top_k(scores, 1)[1][..., 0].astype(jnp.int32)
    linked = jnp.where(jnp.any(matching, axis=-1), chosen, -1).astype(jnp.int32)
    return (levels, linked)


def draw_levels(key, part):
    return index_table(key)[0]


def draw_neighbours(key, part):
    return index_table(key)[1]


def draw_coupling(key, part):
    first_key, second_key = jax.random.split(jax.random.fold_in(key, 11))
    spread = jax.random.uniform(first_key, (PAIRS, 3, 3), jnp.float32, -0.3, 0.3)
    offdiag = 0.5 * (spread + jnp.swapaxes(spread, 1, 2))
    mainly = jax.random.uniform(second_key, (PAIRS, 3), jnp.float32, 0.8, 1.6)
    identity = jnp.eye(3, dtype=jnp.float32)
    return offdiag * (1.0 - identity) + mainly[:, :, None] * identity


def draw_forcing(key, part):
    keys = jax.random.split(jax.random.fold_in(key, 23), 6)
    shape = (PAIRS, 3, ZMAX, Y, XMAX)
    blocks = ZMAX // ZD
    noise = jnp.clip(jax.random.normal(keys[0], shape, jnp.float32), -4.0, 4.0)
    amplitude = jnp.exp(jax.random.uniform(keys[1], (PAIRS, 1, blocks, 1, 1), jnp.float32, -1.09, 1.09))
    share = jax.random.uniform(keys[2], (PAIRS, 1, blocks, 1, 1), jnp.float32, 0.0, 1.0)
    modes = 6
    magnitude = jax.random.randint(keys[3], (PAIRS, 3, modes, 3), 1, 4, dtype=jnp.int32)
    flipping = 2 * jax.random.randint(keys[4], (PAIRS, 3, modes, 3), 0, 2, dtype=jnp.int32) - 1
    wave = (magnitude * flipping).astype(jnp.float32)
    phase = jax.random.uniform(keys[5], (PAIRS, 3, modes), jnp.float32, 0.0, 2.0 * math.pi)
    along_x = (jnp.arange(XMAX, dtype=jnp.float32) + 0.5) / XMAX
    along_y = (jnp.arange(Y, dtype=jnp.float32) + 0.5) / Y
    along_z = (jnp.arange(ZMAX, dtype=jnp.float32) + 0.5) / ZMAX
    smooth = jnp.zeros(shape, jnp.float32)
    for mode in range(modes):
        angle = wave[:, :, mode, 0][:, :, None, None, None] * along_x[None, None, None, None, :] + wave[:, :, mode, 1][:, :, None, None, None] * along_y[None, None, None, :, None] + wave[:, :, mode, 2][:, :, None, None, None] * along_z[None, None, :, None, None]
        smooth = smooth + jnp.cos(2.0 * math.pi * angle + phase[:, :, mode][:, :, None, None, None])
    smooth = smooth * math.sqrt(2.0 / modes)
    share_rows = jnp.repeat(share, ZD, axis=2)
    amplitude_rows = jnp.repeat(amplitude, ZD, axis=2)
    mixed_field = jnp.sqrt(1.0 - share_rows) * noise + jnp.sqrt(share_rows) * smooth
    return jnp.clip(amplitude_rows * mixed_field, -18.0, 18.0)


def block_scale(stream_key, dims, pieces, low, high):
    loudness, own = 1.0, jax.random.fold_in(stream_key, 6)
    for dim, shards_of in pieces:
        heights = jnp.exp(jax.random.uniform(jax.random.fold_in(own, dim), (shards_of,), jnp.float32, low / len(pieces), high / len(pieces)))
        loudness = loudness * jnp.repeat(heights, dims[dim] // shards_of).reshape([-1 if axis == dim else 1 for axis in range(len(dims))])
    return loudness


def setup_inputs(seed: int = 0) -> dict:
    seeds = jax.random.split(jax.random.key(seed), 7)
    forcing = draw_forcing(jax.random.fold_in(seeds[6], 71), 0)
    stiffness = jnp.clip(jnp.exp(math.log(4.0) - 2.7725887 * jax.random.uniform(seeds[1], (PAIRS, 3, ZMAX, Y, XMAX), jnp.float32) ** block_scale(seeds[1], (PAIRS, 3, ZMAX, Y, XMAX), ((0, 4), (2, 8)), -0.2, 0.2)), 0.25, 4.0)
    anisotropy = jnp.clip(jnp.exp(math.log(3.0) - 2.3025851 * jax.random.uniform(seeds[2], (PAIRS, 3, 3), jnp.float32) ** block_scale(seeds[2], (PAIRS, 3, 3), ((0, 4),), -0.2, 0.2)), 0.3, 3.0)
    coupling = draw_coupling(jax.random.fold_in(seeds[6], 71), 0)
    levels = draw_levels(jax.random.fold_in(seeds[6], 71), 0)
    neighbours = draw_neighbours(jax.random.fold_in(seeds[6], 71), 0)
    return {"forcing": forcing, "stiffness": stiffness, "anisotropy": anisotropy, "coupling": coupling, "levels": levels, "neighbours": neighbours}


def level_factor(level_ids):
    return jnp.where(level_ids == 0, 4, jnp.where(level_ids == 1, 2, 1)).astype(jnp.int32)


def resolution(pair_level):
    cells_x = XMAX // level_factor(pair_level[0])
    run_z = ZD // level_factor(pair_level[1])
    return cells_x, run_z, run_z * N_SLAB


def step_up(values, axis_dim):
    length = values.shape[axis_dim]
    widths = [(0, 0)] * values.ndim
    widths[axis_dim] = (0, 1)
    return lax.slice_in_dim(jnp.pad(values, widths), 1, length + 1, axis=axis_dim)


def step_down(values, axis_dim):
    length = values.shape[axis_dim]
    widths = [(0, 0)] * values.ndim
    widths[axis_dim] = (1, 0)
    return lax.slice_in_dim(jnp.pad(values, widths), 0, length, axis=axis_dim)


def to_grid(stored, run_z):
    row_index = jnp.arange(ZMAX, dtype=jnp.int32)
    source = jnp.minimum((row_index // run_z) * ZD + row_index % run_z, ZMAX - 1)
    return jnp.take(stored, source, axis=1)


def from_grid(grid, run_z):
    row_index = jnp.arange(ZMAX, dtype=jnp.int32)
    inner = row_index % ZD
    source = jnp.minimum((row_index // ZD) * run_z + inner, ZMAX - 1)
    keeping = (inner < run_z).astype(jnp.float32)
    return jnp.take(grid, source, axis=1) * keeping[None, :, None, None]


def operate(values, face_list, coefficient, coupling, active):
    result = jnp.sum(coupling[:, :, None, None, None] * values[None], axis=1)
    for facing in range(3):
        axis_dim = 3 - facing
        upper_face, lower_face = face_list[facing]
        result = result + coefficient[:, facing, None, None, None] * (
            upper_face * (values - step_up(values, axis_dim)) + lower_face * (values - step_down(values, axis_dim)))
    return result * active


def solve_pair(operands):
    forcing, stiffness, anisotropy, coupling, pair_level = operands
    cells_x, run_z, depth_z = resolution(pair_level)
    row_index = jnp.arange(ZMAX, dtype=jnp.int32)
    col_index = jnp.arange(XMAX, dtype=jnp.int32)
    active = ((row_index < depth_z)[:, None, None] & (col_index < cells_x)[None, None, :]).astype(jnp.float32)
    source = to_grid(forcing, run_z) * active
    stiff_grid = to_grid(stiffness, run_z) * active
    scales = jnp.stack([(cells_x.astype(jnp.float32) / Y) ** 2, jnp.ones((), jnp.float32),
                        (depth_z.astype(jnp.float32) / Y) ** 2])
    coefficient = anisotropy * scales[None, :]
    diagonal = jnp.diagonal(coupling)[:, None, None, None]
    face_list = []
    for facing in range(3):
        axis_dim = 3 - facing
        single = stiff_grid[facing:facing + 1]
        upper_face = 0.5 * (single + step_up(single, axis_dim))
        lower_face = 0.5 * (single + step_down(single, axis_dim))
        face_list.append((upper_face, lower_face))
        diagonal = diagonal + coefficient[:, facing, None, None, None] * (upper_face + lower_face)
    residual = source
    precond = residual / diagonal
    search = precond
    solution = jnp.zeros_like(source)
    rz_now = jnp.sum(residual * precond)
    for iteration in range(ITERS):
        applied = operate(search, face_list, coefficient, coupling, active)
        step_size = rz_now / jnp.sum(search * applied)
        solution = solution + step_size * search
        if iteration + 1 < ITERS:
            residual = residual - step_size * applied
            precond = residual / diagonal
            rz_next = jnp.sum(residual * precond)
            search = precond + (rz_next / rz_now) * search
            rz_now = rz_next
    return solution


def two_tap(values, axis_dim, fine, coarse):
    length = values.shape[axis_dim]
    ratio = jnp.maximum(fine // jnp.maximum(coarse, 1), 1)
    cells = jnp.arange(length, dtype=jnp.int32)
    numer = 2 * cells + 1 - ratio
    lowest = jnp.floor_divide(numer, 2 * ratio)
    fraction = (numer - lowest * 2 * ratio).astype(jnp.float32) / (2 * ratio).astype(jnp.float32)
    shaped = [1] * values.ndim
    shaped[axis_dim] = length

    def picked(position):
        valid = ((position >= 0) & (position < coarse)).astype(jnp.float32)
        taken = jnp.take(values, jnp.clip(position, 0, length - 1), axis=axis_dim)
        return taken * valid.reshape(shaped)

    result = (1.0 - fraction).reshape(shaped) * picked(lowest) + fraction.reshape(shaped) * picked(lowest + 1)
    return result * (cells < fine).astype(jnp.float32).reshape(shaped)


def interpolate(values, level_from, level_to):
    x_from, run_from, depth_from = resolution(level_from)
    x_to, run_to, depth_to = resolution(level_to)
    moved = two_tap(values, 3, x_to, x_from)
    return two_tap(moved, 1, depth_to, depth_from)


def reference(forcing, stiffness, anisotropy, coupling, levels, neighbours):
    solved = lax.map(solve_pair, (forcing, stiffness, anisotropy, coupling, levels))

    def mix_pair(position):
        pair_level = levels[position]
        link_ids = neighbours[position]
        result = interpolate(solved[position], pair_level, pair_level)
        for entry, weight_sign in ((0, -1.0), (1, -1.0), (2, 1.0)):
            other_id = jnp.maximum(link_ids[entry], 0)
            other_term = interpolate(solved[other_id], levels[other_id], pair_level)
            result = result + (weight_sign * (link_ids[entry] >= 0).astype(jnp.float32)) * other_term
        return from_grid(result, resolution(pair_level)[1])

    return lax.map(mix_pair, jnp.arange(PAIRS, dtype=jnp.int32))
```

```python
import functools

import jax
import jax.numpy as jnp
from jax import lax
from jax.experimental import pallas as pl
from jax.experimental.pallas import tpu as pltpu
from jax.sharding import PartitionSpec as P

CHUNK = 32
PAD = 8
VMEM_SPEC = pl.BlockSpec(memory_space=pltpu.VMEM)
SMEM_SPEC = pl.BlockSpec(memory_space=pltpu.SMEM)
ANY_SPEC = pl.BlockSpec(memory_space=pl.ANY)
f32 = jnp.float32


def shape_of(*dims):
    return jax.ShapeDtypeStruct(dims, f32)


def estimate(flops, nbytes):
    return pl.CostEstimate(flops=int(flops), bytes_accessed=int(nbytes), transcendentals=0)


def cells(full, level):
    return lax.shift_right_logical(jnp.int32(full), 2 - level)


def lanes(rows, width):
    return lax.broadcasted_iota(jnp.int32, (rows, width), 1)


def coefficients(an, nx, nz, height):
    wx = nx.astype(f32) / height
    wz = nz.astype(f32) / height
    wx, wz = wx * wx, wz * wz
    return [[an[c, 0] * wx, an[c, 1], an[c, 2] * wz] for c in range(3)]


def fold(values):
    rows = values.shape[0]
    total = values[0:8]
    for start in range(8, rows, 8):
        total = total + values[start : start + 8]
    return total


def rims_kernel(lev, f_hbm, k_hbm, up, dn, sems):
    depth = f_hbm.shape[1]
    a = cells(depth, lev[lax.axis_index("grp"), 1])
    copies = [
        (f_hbm.at[:, a - 1], up.at[0:3]),
        (k_hbm.at[:, a - 1], up.at[3:6]),
        (k_hbm.at[2, a - 2], up.at[6]),
        (f_hbm.at[:, 0], dn.at[0:3]),
        (k_hbm.at[:, 0], dn.at[3:6]),
        (k_hbm.at[2, 1], dn.at[6]),
    ]
    started = [pltpu.make_async_copy(s, d, sems.at[i]) for i, (s, d) in enumerate(copies)]
    for copy in started:
        copy.start()
    for copy in started:
        copy.wait()


def first_kernel(slabs, lev, an, cp, f, k, lo, hi, zs, w, wl, gx, gys, gz, gl, dots, rj, kys, kzs):
    _, depth, height, width = f.shape
    g = lax.axis_index("grp")
    nx = cells(width, lev[g, 0])
    a = cells(depth, lev[g, 1])
    co = coefficients(an, nx, a * slabs, height)
    lane = lanes(CHUNK, width)
    in_x = lane < nx
    in_xp = lane < nx - 1
    in_xm = lane > 0
    chunks = range(0, height, CHUNK)
    zero_pad = jnp.zeros((PAD, width), f32)

    def keep(values):
        return jnp.where(in_x, values, 0.0)

    def pad_row(row):
        kys[row, 0:PAD] = zero_pad
        kys[row, height + PAD :] = zero_pad
        for c in range(3):
            zs[c, row, 0:PAD] = zero_pad
            zs[c, row, height + PAD :] = zero_pad

    def stage(row, _):
        pad_row(row + 1)
        for y in chunks:
            kys[row + 1, PAD + y : PAD + y + CHUNK] = keep(k[1, row, y : y + CHUNK])
            kzs[row + 2, y : y + CHUNK] = keep(k[2, row, y : y + CHUNK])
        return 0

    lax.fori_loop(0, a, stage, 0)
    pad_row(0)
    pad_row(a + 1)
    for y in chunks:
        here = slice(y, y + CHUNK)
        kys[0, PAD + y : PAD + y + CHUNK] = keep(lo[4, here])
        kys[a + 1, PAD + y : PAD + y + CHUNK] = keep(hi[4, here])
        kzs[0, here] = keep(lo[6, here])
        kzs[1, here] = keep(lo[5, here])
        kzs[a + 2, here] = keep(hi[5, here])
        kzs[a + 3, here] = keep(hi[6, here])

    def jacobi(f_at, kx_at, row, own):
        for y in chunks:
            kx = keep(kx_at(y))
            kxp = jnp.where(in_xp, pltpu.roll(kx, width - 1, 1), 0.0)
            kxm = jnp.where(in_xm, pltpu.roll(kx, 1, 1), 0.0)
            ky = kys[row, PAD + y : PAD + y + CHUNK]
            kyp = kys[row, PAD + y + 1 : PAD + y + 1 + CHUNK]
            kym = kys[row, PAD + y - 1 : PAD + y - 1 + CHUNK]
            kz = kzs[row + 1, y : y + CHUNK]
            kzp = kzs[row + 2, y : y + CHUNK]
            kzm = kzs[row, y : y + CHUNK]
            sx = kx + 0.5 * (kxp + kxm)
            sy = ky + 0.5 * (kyp + kym)
            sz = kz + 0.5 * (kzp + kzm)
            for c in range(3):
                diagonal = cp[c, c] + co[c][0] * sx + co[c][1] * sy + co[c][2] * sz
                inverse = 1.0 / diagonal
                zs[c, row, PAD + y : PAD + y + CHUNK] = keep(f_at(c, y)) * inverse
                if own:
                    rj[c, row - 1, y : y + CHUNK] = inverse
            if own:
                gx[row - 1, y : y + CHUNK] = jnp.where(in_xp, 0.5 * (kx + kxp), 0.0)
                gys[row - 1, PAD + y : PAD + y + CHUNK] = 0.5 * (ky + kyp)
                gz[row - 1, y : y + CHUNK] = 0.5 * (kz + kzp)

    def own_row(row, _):
        gys[row, 0:PAD] = zero_pad
        jacobi(
            lambda c, y: f[c, row, y : y + CHUNK], lambda y: k[0, row, y : y + CHUNK], row + 1, True
        )
        return 0

    jacobi(lambda c, y: lo[c, y : y + CHUNK], lambda y: lo[3, y : y + CHUNK], 0, False)
    jacobi(lambda c, y: hi[c, y : y + CHUNK], lambda y: hi[3, y : y + CHUNK], a + 1, False)
    lax.fori_loop(0, a, own_row, 0)
    for y in chunks:
        gl[y : y + CHUNK] = 0.5 * (kzs[1, y : y + CHUNK] + kzs[2, y : y + CHUNK])

    def image_row(row, sums):
        s0, s1, s2 = sums
        for c in range(3):
            w[c, row, height:] = zero_pad
        for y in chunks:
            here = slice(y, y + CHUNK)
            mid = slice(PAD + y, PAD + y + CHUNK)
            above = slice(PAD + y + 1, PAD + y + 1 + CHUNK)
            below = slice(PAD + y - 1, PAD + y - 1 + CHUNK)
            fx = gx[row, here]
            fyp, fym = gys[row, mid], gys[row, below]
            fzp = gz[row, here]
            fzm = 0.5 * (kzs[row + 1, here] + kzs[row + 2, here])
            z = [zs[c, row + 1, mid] for c in range(3)]
            for c in range(3):
                tx = fx * pltpu.roll(z[c], width - 1, 1) + pltpu.roll(fx * z[c], 1, 1)
                ty = fyp * zs[c, row + 1, above] + fym * zs[c, row + 1, below]
                tz = fzp * zs[c, row + 2, mid] + fzm * zs[c, row, mid]
                v = co[c][0] * tx + co[c][1] * ty + co[c][2] * tz
                for other in range(3):
                    if other != c:
                        v = v - cp[c, other] * z[other]
                force = keep(f[c, row, here])
                image = force - v
                scaled = z[c] - v * rj[c, row, here]
                w[c, row, here] = scaled
                s0 = s0 + fold(force * z[c])
                s1 = s1 + fold(image * z[c])
                s2 = s2 + fold(image * scaled)
        return s0, s1, s2

    nothing = jnp.zeros((8, width), f32)
    s0, s1, s2 = lax.fori_loop(0, a, image_row, (nothing, nothing, nothing))
    for c in range(3):
        for y in chunks:
            wl[c, y : y + CHUNK] = w[c, a - 1, y : y + CHUNK]
    dots[...] = jnp.zeros((8, width), f32)
    for i, total in enumerate((s0, s1, s2)):
        dots[i : i + 1, :] = jnp.sum(total, axis=0, keepdims=True)


def second_kernel(slabs, lev, an, cp, w, gx, gys, gz, part):
    depth, height, width = gx.shape
    g = lax.axis_index("grp")
    nx = cells(width, lev[g, 0])
    a = cells(depth, lev[g, 1])
    co = coefficients(an, nx, a * slabs, height)

    def row_sum(row, total, inner):
        for y in range(0, height, CHUNK):
            here = slice(y, y + CHUNK)
            fx, fy = gx[row, here], gys[row, PAD + y : PAD + y + CHUNK]
            fz = gz[row, here] if inner else None
            own = [w[c, row, here] for c in range(3)]
            for c in range(3):
                v = co[c][0] * (fx * pltpu.roll(own[c], width - 1, 1))
                v = v + co[c][1] * (fy * w[c, row, y + 1 : y + 1 + CHUNK])
                if inner:
                    v = v + co[c][2] * (fz * w[c, row + 1, here])
                if c < 2:
                    v = v - cp[c, c + 1] * own[c + 1]
                if c == 0:
                    v = v - cp[0, 2] * own[2]
                total = total + fold(v * own[c])
        return total

    total = lax.fori_loop(
        0, a - 1, lambda row, t: row_sum(row, t, True), jnp.zeros((8, width), f32)
    )
    part[...] = 2.0 * row_sum(a - 1, total, False)


def cross_kernel(slabs, lev, an, w, gl, wlo, part, dots, out):
    depth, height, width = w.shape[1], gl.shape[0], gl.shape[1]
    g = lax.axis_index("grp")
    nx = cells(width, lev[g, 0])
    a = cells(depth, lev[g, 1])
    co = coefficients(an, nx, a * slabs, height)
    total = jnp.zeros((8, width), f32)
    for y in range(0, height, CHUNK):
        here = slice(y, y + CHUNK)
        v = jnp.zeros((CHUNK, width), f32)
        for c in range(3):
            v = v + co[c][2] * (w[c, 0, here] * wlo[c, here])
        total = total + fold(gl[here] * v)
    out[...] = dots[...]
    out[3:4, :] = jnp.sum(part[...] + 2.0 * total, axis=0, keepdims=True)


def solution_kernel(lev, mine, theirs, zs, w, u, h1, h2):
    _, depth, height, width = u.shape
    half = depth // 2
    quarter = half // 2
    g = lax.axis_index("grp")
    a = cells(depth, lev[g, 1])
    narrow = lev[g, 0] < 2
    sums = jnp.sum(mine[...] + theirs[...], axis=1, keepdims=True)
    sums = jnp.broadcast_to(sums, (8, width))
    d0, d1, d2, e3 = sums[0:1], sums[1:2], sums[2:3], sums[3:4]
    d3 = d2 - e3
    first = d0 / d1
    rz = first * first * d2 - d0
    more = 1.0 + rz / d0
    bend = more * more * d1 - 2.0 * first * more * d2 + first * first * d3
    second = rz / bend
    alpha = jnp.broadcast_to(first + second * more, (CHUNK, width))
    beta = jnp.broadcast_to(-second * first, (CHUNK, width))
    chunks = range(0, height, CHUNK)

    def active_row(row, _):
        for c in range(3):
            for y in chunks:
                z = zs[c, row + 1, PAD + y : PAD + y + CHUNK]
                u[c, row, y : y + CHUNK] = alpha * z + beta * w[c, row, y : y + CHUNK]
        return 0

    def idle_row(row, _):
        for c in range(3):
            for y in chunks:
                u[c, row, y : y + CHUNK] = jnp.zeros((CHUNK, width), f32)
        return 0

    lax.fori_loop(0, a, active_row, 0)
    lax.fori_loop(a, depth, idle_row, 0)
    share = jnp.where(narrow, 1.0, 0.0)
    for n in range(half):
        target, slot = (h1, n) if n < quarter else (h2, n - quarter)
        for c in range(3):
            for y in chunks:
                here = slice(y, y + CHUNK)
                beside = pltpu.roll(u[c, n + half, here], width // 2, 1)
                target[c, slot, here] = u[c, n, here] + share * beside


def role(lev, nb, g, p):
    n0, n1, n2 = nb[g, 0], nb[g, 1], nb[g, 2]
    sign = jnp.where(n2 == p, 1.0, 0.0) - jnp.where((n0 == p) | (n1 == p), 1.0, 0.0)
    coarse = lev[p, 1] < lev[g, 1]
    return sign.astype(f32), coarse


def x_weights(lev, g, p, sign, width):
    to_x = cells(width, lev[g, 0])
    from_x = cells(width, lev[p, 0])
    source = lax.broadcasted_iota(jnp.int32, (width, 2 * width), 0)
    target = lax.broadcasted_iota(jnp.int32, (width, 2 * width), 1)
    second = target >= width
    target = jnp.where(second, target - width, target)
    shift = jnp.where(second, width // 2, 0)
    cell = source - shift
    ratio = from_x.astype(f32) / to_x.astype(f32)
    along = (target.astype(f32) + 0.5) * ratio
    weight = jnp.maximum(0.0, 1.0 - jnp.abs(along - (cell.astype(f32) + 0.5)))
    fits = (target < to_x) & (cell >= 0) & (cell < from_x)
    fits = fits & (jnp.logical_not(second) | (lev[p, 0] < 2))
    return jnp.where(fits, weight * sign, 0.0).astype(jnp.bfloat16)


def split_dot(values, weights):
    high = values.astype(jnp.bfloat16)
    rest = values - high.astype(f32)
    middle = rest.astype(jnp.bfloat16)
    low = (rest - middle.astype(f32)).astype(jnp.bfloat16)
    dot = functools.partial(jnp.dot, preferred_element_type=f32)
    return dot(high, weights) + (dot(middle, weights) + dot(low, weights))


def edges_kernel(others, lev, nb, *refs):
    pieces = refs[: 2 * len(others)]
    up, dn, weights = refs[2 * len(others) :]
    _, quarter, height, width = pieces[0].shape
    depth = 4 * quarter
    g = lax.axis_index("grp")
    up[...] = jnp.zeros(up.shape, f32)
    dn[...] = jnp.zeros(dn.shape, f32)
    for i, other in enumerate(others):
        h1, h2 = pieces[2 * i], pieces[2 * i + 1]
        p = other(g)
        sign, coarse = role(lev, nb, g, p)

        @pl.when((sign != 0.0) & coarse)
        def _():
            weights[...] = x_weights(lev, g, p, sign, width)[:, :width]
            last = cells(depth, lev[p, 1]) - 1
            in_first = last < quarter
            i1 = jnp.minimum(last, quarter - 1)
            i2 = jnp.maximum(last - quarter, 0)
            for c in range(3):
                dn[c] += 0.25 * split_dot(h1[c, 0], weights[...])
                row = jnp.where(in_first, h1[c, i1], h2[c, i2])
                up[c] += 0.25 * split_dot(row, weights[...])


def mix_kernel(others, lev, nb, u, *refs):
    pieces = refs[: 2 * len(others)]
    out, weights = refs[2 * len(others) :]
    _, depth, height, width = u.shape
    half = depth // 2
    quarter = half // 2
    g = lax.axis_index("grp")
    run = cells(depth, lev[g, 1])
    for c in range(3):
        for row in range(depth):
            out[c, row] = u[c, row]
    for i, other in enumerate(others):
        p = other(g)
        sign, coarse = role(lev, nb, g, p)

        def plane(c, n):
            ref, slot = (pieces[2 * i], n) if n < quarter else (pieces[2 * i + 1], n - quarter)
            return ref[c, slot]

        @pl.when(sign != 0.0)
        def _():
            weights[...] = x_weights(lev, g, p, sign, width)

        @pl.when((sign != 0.0) & jnp.logical_not(coarse))
        def _():
            def component(c, _):
                for n in range(half):
                    both = split_dot(plane(c, n), weights[...])
                    out[c, n] += both[:, :width]
                    out[c, n + half] += both[:, width:]
                return 0

            lax.fori_loop(0, 3, component, 0)

        @pl.when((sign != 0.0) & coarse)
        def _():
            def component(c, _):
                for n in range(half):
                    one = split_dot(plane(c, n), weights[:, :width])
                    out[c, 2 * n] += 0.75 * one
                    out[c, 2 * n + 1] += 0.75 * one
                    if n > 0:
                        out[c, 2 * n - 1] += 0.25 * one
                    if n < half - 1:
                        share = jnp.where(2 * n + 2 < run, 0.25, 0.0)
                        out[c, 2 * n + 2] += share * one
                return 0

            lax.fori_loop(0, 3, component, 0)


def finish_kernel(lev, lo, hi, given, out, first, last, sems):
    depth = out.shape[1]
    run = cells(depth, lev[lax.axis_index("grp"), 1])
    reads = [
        pltpu.make_async_copy(given.at[:, 0], first, sems.at[0]),
        pltpu.make_async_copy(given.at[:, run - 1], last, sems.at[1]),
    ]
    for copy in reads:
        copy.start()
    for copy in reads:
        copy.wait()
    first[...] += lo[...]
    last[...] += hi[...]
    writes = [
        pltpu.make_async_copy(first, out.at[:, 0], sems.at[0]),
        pltpu.make_async_copy(last, out.at[:, run - 1], sems.at[1]),
    ]
    for copy in writes:
        copy.start()
    for copy in writes:
        copy.wait()


def permute_up(values):
    slabs = lax.axis_size("slab")
    return lax.ppermute(values, "slab", [(i, i + 1) for i in range(slabs - 1)])


def permute_down(values):
    slabs = lax.axis_size("slab")
    return lax.ppermute(values, "slab", [(i + 1, i) for i in range(slabs - 1)])


def along(values, axis, step):
    peers = lax.axis_size(axis)
    return lax.ppermute(values, axis, [(i, i ^ step) for i in range(peers)])


def slab_sums(sums):
    slabs = lax.axis_size("slab")
    step = 1
    while 2 * step < slabs:
        sums = sums + along(sums, "slab", step)
        step *= 2
    return sums, along(sums, "slab", step)


def gather(h1, h2):
    groups = lax.axis_size("grp")
    if groups == 4:
        a1, b2 = along(h1, "grp", 1), along(h2, "grp", 2)
        a2, b1 = along(h2, "grp", 1), along(h1, "grp", 2)
        c1, c2 = along(a1, "grp", 2), along(b2, "grp", 1)
        return [(1, a1, a2), (2, b1, b2), (3, c1, c2)]
    return [(step, along(h1, "grp", step), along(h2, "grp", step)) for step in range(1, groups)]


def call(kernel, outs, specs_in, specs_out, scratch=(), cost=None, **more):
    return pl.pallas_call(
        kernel,
        out_shape=outs,
        in_specs=specs_in,
        out_specs=specs_out,
        scratch_shapes=list(scratch),
        cost_estimate=cost,
        **more,
    )


def per_device(forcing, stiffness, anisotropy, coupling, levels, neighbours):
    _, _, depth, height, width = forcing.shape
    slabs = lax.axis_size("slab")
    quarter = depth // 4
    f, k = forcing[0], stiffness[0]
    an, cp = anisotropy[0], coupling[0]
    plane = 4 * height * width
    padded = height + 2 * PAD
    dma = pltpu.SemaphoreType.DMA

    up, dn = call(
        rims_kernel,
        [shape_of(7, height, width)] * 2,
        [SMEM_SPEC, ANY_SPEC, ANY_SPEC],
        [VMEM_SPEC] * 2,
        [dma((6,))],
        estimate(0, 28 * plane),
        name="rims",
    )(levels, f, k)
    lo, hi = permute_up(up), permute_down(dn)

    zs, w, wl, gx, gys, gz, gl, dots = call(
        functools.partial(first_kernel, slabs),
        [
            shape_of(3, depth + 2, padded, width),
            shape_of(3, depth, height + PAD, width),
            shape_of(3, height, width),
            shape_of(depth, height, width),
            shape_of(depth, height + PAD, width),
            shape_of(depth, height, width),
            shape_of(height, width),
            shape_of(8, width),
        ],
        [SMEM_SPEC] * 3 + [VMEM_SPEC] * 4,
        [VMEM_SPEC] * 8,
        [
            pltpu.VMEM((3, depth, height, width), f32),
            pltpu.VMEM((depth + 2, padded, width), f32),
            pltpu.VMEM((depth + 4, height, width), f32),
        ],
        estimate(150 * depth * plane, 150 * plane),
        name="first",
    )(levels, an, cp, f, k, lo, hi)
    wlo = permute_up(wl)
    part = call(
        functools.partial(second_kernel, slabs),
        shape_of(8, width),
        [SMEM_SPEC] * 3 + [VMEM_SPEC] * 4,
        VMEM_SPEC,
        cost=estimate(30 * depth * plane, 50 * plane),
        name="second",
    )(levels, an, cp, w, gx, gys, gz)
    dots = call(
        functools.partial(cross_kernel, slabs),
        shape_of(8, width),
        [SMEM_SPEC] * 2 + [VMEM_SPEC] * 5,
        VMEM_SPEC,
        cost=estimate(8 * plane, 6 * plane),
        name="cross",
    )(levels, an, w, gl, wlo, part, dots)
    mine, theirs = slab_sums(dots)
    u, h1, h2 = call(
        solution_kernel,
        [shape_of(3, depth, height, width)] + [shape_of(3, quarter, height, width)] * 2,
        [SMEM_SPEC] + [VMEM_SPEC] * 4,
        [VMEM_SPEC] * 3,
        cost=estimate(4 * depth * plane, 90 * plane),
        name="solve",
    )(levels, mine, theirs, zs, w)
    received = gather(h1, h2)
    others = [functools.partial(lambda step, g: g ^ step, step) for step, _, _ in received]
    pieces = [piece for _, first, second in received for piece in (first, second)]
    edge_up, edge_dn = call(
        functools.partial(edges_kernel, others),
        [shape_of(3, height, width)] * 2,
        [SMEM_SPEC] * 2 + [VMEM_SPEC] * len(pieces),
        [VMEM_SPEC] * 2,
        [pltpu.VMEM((width, width), jnp.bfloat16)],
        estimate(100 * plane, 40 * plane),
        name="edges",
    )(levels, neighbours, *pieces)
    from_lo, from_hi = permute_up(edge_up), permute_down(edge_dn)
    mixed = call(
        functools.partial(mix_kernel, others),
        shape_of(3, depth, height, width),
        [SMEM_SPEC] * 2 + [VMEM_SPEC] * (1 + len(pieces)),
        VMEM_SPEC,
        [pltpu.VMEM((width, 2 * width), jnp.bfloat16)],
        estimate(2000 * plane, 90 * plane),
        name="mix",
    )(levels, neighbours, u, *pieces)
    mixed = call(
        finish_kernel,
        shape_of(3, depth, height, width),
        [SMEM_SPEC] + [VMEM_SPEC] * 2 + [ANY_SPEC],
        ANY_SPEC,
        [
            pltpu.VMEM((3, height, width), f32),
            pltpu.VMEM((3, height, width), f32),
            dma((2,)),
        ],
        estimate(0, 18 * plane),
        input_output_aliases={3: 0},
        name="finish",
    )(levels, from_lo, from_hi, mixed)
    return mixed[None]


def solution(mesh):
    return jax.shard_map(
        per_device,
        mesh=mesh,
        in_specs=(
            P("grp", None, "slab", None, None),
            P("grp", None, "slab", None, None),
            P("grp", None, None),
            P("grp", None, None),
            P(),
            P(),
        ),
        out_specs=P("grp", None, "slab", None, None),
        check_vma=False,
    )
```

```python
import functools

import jax
import jax.numpy as jnp
from jax import lax
from jax.experimental import pallas as pl
from jax.experimental.pallas import tpu as pltpu
from jax.sharding import PartitionSpec as P

CHUNK = 32
PAD = 8
VMEM_SPEC = pl.BlockSpec(memory_space=pltpu.VMEM)
SMEM_SPEC = pl.BlockSpec(memory_space=pltpu.SMEM)
HBM_SPEC = pl.BlockSpec(memory_space=pltpu.HBM)
VMEM_LIMIT = 18 * 1024 * 1024
f32 = jnp.float32


def shape_of(*dims):
    return jax.ShapeDtypeStruct(dims, f32)


def estimate(flops, nbytes):
    return pl.CostEstimate(flops=int(flops), bytes_accessed=int(nbytes), transcendentals=0)


def cells(full, level):
    return lax.shift_right_logical(jnp.int32(full), 2 - level)


def lanes(rows, width):
    return lax.broadcasted_iota(jnp.int32, (rows, width), 1)


def coefficients(an, nx, nz, height):
    wx = nx.astype(f32) / height
    wz = nz.astype(f32) / height
    wx, wz = wx * wx, wz * wz
    return [[an[c, 0, 0] * wx, an[c, 0, 1], an[c, 0, 2] * wz] for c in range(3)]


def fold(values):
    rows = values.shape[0]
    total = values[0:8]
    for start in range(8, rows, 8):
        total = total + values[start : start + 8]
    return total


def rims_kernel(lev, f_hbm, k_hbm, one, two, sems):
    depth = f_hbm.shape[1]
    a = cells(depth, lev[1, lax.axis_index("grp")])
    even = lax.rem(lax.axis_index("slab"), 2) == 0
    started = []
    for i, (rows, last) in enumerate(((one, even), (two, jnp.logical_not(even)))):
        near = jnp.where(last, a - 1, 0)
        far = jnp.where(last, a - 2, 1)
        for j, (source, target) in enumerate(
            (
                (f_hbm.at[:, near], rows.at[0:3]),
                (k_hbm.at[:, near], rows.at[3:6]),
                (k_hbm.at[2, far], rows.at[6]),
            )
        ):
            started.append(pltpu.make_async_copy(source, target, sems.at[3 * i + j]))
    for copy in started:
        copy.start()
    for copy in started:
        copy.wait()


def first_kernel(
    slabs, lev, an, cp, f, k, one, two, zs, w, wl, w0, gx, gys, gz, gl, dots, rj, kys, kzs
):
    _, depth, height, width = f.shape
    g = lax.axis_index("grp")
    nx = cells(width, lev[0, g])
    a = cells(depth, lev[1, g])
    co = coefficients(an, nx, a * slabs, height)
    lane = lanes(CHUNK, width)
    in_x = lane < nx
    in_xp = lane < nx - 1
    in_xm = lane > 0
    chunks = range(0, height, CHUNK)
    zero_pad = jnp.zeros((PAD, width), f32)

    def keep(values):
        return jnp.where(in_x, values, 0.0)

    def pad_row(row):
        kys[row, 0:PAD] = zero_pad
        kys[row, height + PAD :] = zero_pad
        for c in range(3):
            zs[c, row, 0:PAD] = zero_pad
            zs[c, row, height + PAD :] = zero_pad

    def stage(row, _):
        pad_row(row + 1)
        for y in chunks:
            kys[row + 1, PAD + y : PAD + y + CHUNK] = keep(k[1, row, y : y + CHUNK])
            kzs[row + 2, y : y + CHUNK] = keep(k[2, row, y : y + CHUNK])
        return 0

    lax.fori_loop(0, a, stage, 0)
    pad_row(0)
    pad_row(a + 1)
    even = lax.rem(lax.axis_index("slab"), 2) == 0
    rims = []
    for rows, above in ((one, even), (two, jnp.logical_not(even))):
        at = jnp.where(above, a + 1, 0)
        near = jnp.where(above, a + 2, 1)
        far = jnp.where(above, a + 3, 0)
        rims.append((rows, at))
        for y in chunks:
            here = slice(y, y + CHUNK)
            kys[at, PAD + y : PAD + y + CHUNK] = keep(rows[4, here])
            kzs[near, here] = keep(rows[5, here])
            kzs[far, here] = keep(rows[6, here])

    def jacobi(f_at, kx_at, row, own):
        for y in chunks:
            kx = keep(kx_at(y))
            kxp = jnp.where(in_xp, pltpu.roll(kx, width - 1, 1), 0.0)
            kxm = jnp.where(in_xm, pltpu.roll(kx, 1, 1), 0.0)
            ky = kys[row, PAD + y : PAD + y + CHUNK]
            kyp = kys[row, PAD + y + 1 : PAD + y + 1 + CHUNK]
            kym = kys[row, PAD + y - 1 : PAD + y - 1 + CHUNK]
            kz = kzs[row + 1, y : y + CHUNK]
            kzp = kzs[row + 2, y : y + CHUNK]
            kzm = kzs[row, y : y + CHUNK]
            sx = kx + 0.5 * (kxp + kxm)
            sy = ky + 0.5 * (kyp + kym)
            sz = kz + 0.5 * (kzp + kzm)
            for c in range(3):
                diagonal = cp[c, 0, c] + co[c][0] * sx + co[c][1] * sy + co[c][2] * sz
                inverse = 1.0 / diagonal
                zs[c, row, PAD + y : PAD + y + CHUNK] = keep(f_at(c, y)) * inverse
                if own:
                    rj[c, row - 1, y : y + CHUNK] = inverse
            if own:
                gx[row - 1, y : y + CHUNK] = jnp.where(in_xp, 0.5 * (kx + kxp), 0.0)
                gys[row - 1, PAD + y : PAD + y + CHUNK] = 0.5 * (ky + kyp)
                gz[row - 1, y : y + CHUNK] = 0.5 * (kz + kzp)

    def own_row(row, _):
        gys[row, 0:PAD] = zero_pad
        jacobi(
            lambda c, y: f[c, row, y : y + CHUNK], lambda y: k[0, row, y : y + CHUNK], row + 1, True
        )
        return 0

    for rows, at in rims:
        jacobi(
            lambda c, y: rows[c, y : y + CHUNK], lambda y: rows[3, y : y + CHUNK], at, False
        )
    lax.fori_loop(0, a, own_row, 0)
    for y in chunks:
        gl[y : y + CHUNK] = 0.5 * (kzs[1, y : y + CHUNK] + kzs[2, y : y + CHUNK])

    def image_row(row, sums):
        s0, s1, s2 = sums
        for c in range(3):
            w[c, row, height:] = zero_pad
        for y in chunks:
            here = slice(y, y + CHUNK)
            mid = slice(PAD + y, PAD + y + CHUNK)
            above = slice(PAD + y + 1, PAD + y + 1 + CHUNK)
            below = slice(PAD + y - 1, PAD + y - 1 + CHUNK)
            fx = gx[row, here]
            fyp, fym = gys[row, mid], gys[row, below]
            fzp = gz[row, here]
            fzm = 0.5 * (kzs[row + 1, here] + kzs[row + 2, here])
            z = [zs[c, row + 1, mid] for c in range(3)]
            for c in range(3):
                tx = fx * pltpu.roll(z[c], width - 1, 1) + pltpu.roll(fx * z[c], 1, 1)
                ty = fyp * zs[c, row + 1, above] + fym * zs[c, row + 1, below]
                tz = fzp * zs[c, row + 2, mid] + fzm * zs[c, row, mid]
                v = co[c][0] * tx + co[c][1] * ty + co[c][2] * tz
                for other in range(3):
                    if other != c:
                        v = v - cp[c, 0, other] * z[other]
                force = keep(f[c, row, here])
                image = force - v
                scaled = z[c] - v * rj[c, row, here]
                w[c, row, here] = scaled
                s0 = s0 + fold(force * z[c])
                s1 = s1 + fold(image * z[c])
                s2 = s2 + fold(image * scaled)
        return s0, s1, s2

    nothing = jnp.zeros((8, width), f32)
    s0, s1, s2 = lax.fori_loop(0, a, image_row, (nothing, nothing, nothing))
    for c in range(3):
        for y in chunks:
            wl[c, y : y + CHUNK] = w[c, a - 1, y : y + CHUNK]
            w0[c, y : y + CHUNK] = w[c, 0, y : y + CHUNK]
    dots[...] = jnp.zeros((8, width), f32)
    for i, total in enumerate((s0, s1, s2)):
        dots[i : i + 1, :] = jnp.sum(total, axis=0, keepdims=True)


def second_kernel(slabs, lev, an, cp, w, gx, gys, gz, part):
    depth, height, width = gx.shape
    g = lax.axis_index("grp")
    nx = cells(width, lev[0, g])
    a = cells(depth, lev[1, g])
    co = coefficients(an, nx, a * slabs, height)

    def row_sum(row, total, inner):
        for y in range(0, height, CHUNK):
            here = slice(y, y + CHUNK)
            fx, fy = gx[row, here], gys[row, PAD + y : PAD + y + CHUNK]
            fz = gz[row, here] if inner else None
            own = [w[c, row, here] for c in range(3)]
            for c in range(3):
                v = co[c][0] * (fx * pltpu.roll(own[c], width - 1, 1))
                v = v + co[c][1] * (fy * w[c, row, y + 1 : y + 1 + CHUNK])
                if inner:
                    v = v + co[c][2] * (fz * w[c, row + 1, here])
                if c < 2:
                    v = v - cp[c, 0, c + 1] * own[c + 1]
                if c == 0:
                    v = v - cp[0, 0, 2] * own[2]
                total = total + fold(v * own[c])
        return total

    total = lax.fori_loop(
        0, a - 1, lambda row, t: row_sum(row, t, True), jnp.zeros((8, width), f32)
    )
    part[...] = 2.0 * row_sum(a - 1, total, False)


def cross_kernel(slabs, depth, lev, an, w0, gl, wlo, part, dots, out):
    height, width = gl.shape
    g = lax.axis_index("grp")
    nx = cells(width, lev[0, g])
    a = cells(depth, lev[1, g])
    co = coefficients(an, nx, a * slabs, height)
    total = jnp.zeros((8, width), f32)
    for y in range(0, height, CHUNK):
        here = slice(y, y + CHUNK)
        v = jnp.zeros((CHUNK, width), f32)
        for c in range(3):
            v = v + co[c][2] * (w0[c, here] * wlo[c, here])
        total = total + fold(gl[here] * v)
    out[...] = dots[...]
    out[3:4, :] = jnp.sum(part[...] + 2.0 * total, axis=0, keepdims=True)


def slot_rows(depth, run):
    half, quarter = depth // 2, depth // 4
    last = jnp.where(run == quarter, quarter - 1, half - 1)
    rest = [n for n in range(1, half - 1) if n != quarter - 1]
    return [0, last] + rest + [half + quarter - 2 - last]


def solution_kernel(lev, mine, theirs, zs, w, u, *slots):
    _, depth, height, width = u.shape
    half = depth // 2
    g = lax.axis_index("grp")
    a = cells(depth, lev[1, g])
    narrow = lev[0, g] < 2
    sums = jnp.sum(mine[...] + theirs[...], axis=1, keepdims=True)
    sums = jnp.broadcast_to(sums, (8, width))
    d0, d1, d2, e3 = sums[0:1], sums[1:2], sums[2:3], sums[3:4]
    d3 = d2 - e3
    first = d0 / d1
    rz = first * first * d2 - d0
    more = 1.0 + rz / d0
    bend = more * more * d1 - 2.0 * first * more * d2 + first * first * d3
    second = rz / bend
    alpha = jnp.broadcast_to(first + second * more, (CHUNK, width))
    beta = jnp.broadcast_to(-second * first, (CHUNK, width))
    chunks = range(0, height, CHUNK)

    def active_row(row, _):
        for c in range(3):
            for y in chunks:
                z = zs[c, row + 1, PAD + y : PAD + y + CHUNK]
                u[c, row, y : y + CHUNK] = alpha * z + beta * w[c, row, y : y + CHUNK]
        return 0

    def idle_row(row, _):
        for c in range(3):
            for y in chunks:
                u[c, row, y : y + CHUNK] = jnp.zeros((CHUNK, width), f32)
        return 0

    lax.fori_loop(0, a, active_row, 0)
    lax.fori_loop(a, depth, idle_row, 0)
    share = jnp.where(narrow, 1.0, 0.0)
    for slot, n in zip(slots, slot_rows(depth, a)):
        for c in range(3):
            for y in chunks:
                here = slice(y, y + CHUNK)
                beside = pltpu.roll(u[c, n + half, here], width // 2, 1)
                slot[c, here] = u[c, n, here] + share * beside


def role(lev, nb, g, p):
    n0, n1, n2 = nb[g, 0], nb[g, 1], nb[g, 2]
    sign = jnp.where(n2 == p, 1.0, 0.0) - jnp.where((n0 == p) | (n1 == p), 1.0, 0.0)
    coarse = lev[1, p] < lev[1, g]
    return sign.astype(f32), coarse


def x_weights(lev, g, p, sign, width):
    to_x = cells(width, lev[0, g])
    from_x = cells(width, lev[0, p])
    source = lax.broadcasted_iota(jnp.int32, (width, 2 * width), 0)
    target = lax.broadcasted_iota(jnp.int32, (width, 2 * width), 1)
    second = target >= width
    target = jnp.where(second, target - width, target)
    shift = jnp.where(second, width // 2, 0)
    cell = source - shift
    ratio = from_x.astype(f32) / to_x.astype(f32)
    along = (target.astype(f32) + 0.5) * ratio
    weight = jnp.maximum(0.0, 1.0 - jnp.abs(along - (cell.astype(f32) + 0.5)))
    fits = (target < to_x) & (cell >= 0) & (cell < from_x)
    fits = fits & (jnp.logical_not(second) | (lev[0, p] < 2))
    return jnp.where(fits, weight * sign, 0.0).astype(jnp.bfloat16)


def split_dot(values, weights):
    high = values.astype(jnp.bfloat16)
    rest = values - high.astype(f32)
    middle = rest.astype(jnp.bfloat16)
    low = (rest - middle.astype(f32)).astype(jnp.bfloat16)
    dot = functools.partial(jnp.dot, preferred_element_type=f32)
    return dot(high, weights) + (dot(middle, weights) + dot(low, weights))


def edges_kernel(others, lev, nb, *refs):
    pieces = refs[: 2 * len(others)]
    one, two, weights = refs[2 * len(others) :]
    width = one.shape[2]
    g = lax.axis_index("grp")
    even = lax.rem(lax.axis_index("slab"), 2) == 0
    one[...] = jnp.zeros(one.shape, f32)
    two[...] = jnp.zeros(two.shape, f32)
    for i, other in enumerate(others):
        first, last = pieces[2 * i : 2 * i + 2]
        p = other(g)
        sign, coarse = role(lev, nb, g, p)

        @pl.when((sign != 0.0) & coarse)
        def _():
            weights[...] = x_weights(lev, g, p, sign, width)[:, :width]

            def component(c, _):
                below = 0.25 * split_dot(first[c], weights[...])
                above = 0.25 * split_dot(last[c], weights[...])
                one[c] += jnp.where(even, above, below)
                two[c] += jnp.where(even, below, above)
                return 0

            lax.fori_loop(0, 3, component, 0)


def mix_kernel(others, which, depth, ends, lev, nb, start, *refs):
    pieces = refs[: len(which) * len(others)]
    rims = refs[len(pieces) : len(pieces) + (2 if ends else 0)]
    out, weights = refs[len(pieces) + len(rims) :]
    width = start.shape[3]
    half = depth // 2
    g = lax.axis_index("grp")
    run = cells(depth, lev[1, g])

    def begin(c, _):
        for row in range(depth):
            out[c, row] = start[c, row]
        return 0

    lax.fori_loop(0, 3, begin, 0)
    for i, other in enumerate(others):
        p = other(g)
        sign, coarse = role(lev, nb, g, p)
        slots = pieces[len(which) * i : len(which) * (i + 1)]
        order = slot_rows(depth, cells(depth, lev[1, p]))
        rows = [order[j] for j in which]

        @pl.when(sign != 0.0)
        def _():
            weights[...] = x_weights(lev, g, p, sign, width)

        @pl.when((sign != 0.0) & jnp.logical_not(coarse))
        def _():
            def component(c, _):
                for n, slot in zip(rows, slots):
                    both = split_dot(slot[c], weights[...])
                    out[c, n] += both[:, :width]
                    out[c, n + half] += both[:, width:]
                return 0

            lax.fori_loop(0, 3, component, 0)

        @pl.when((sign != 0.0) & coarse)
        def _():
            def component(c, _):
                for n, slot in zip(rows, slots):
                    one = split_dot(slot[c], weights[:, :width])
                    out[c, 2 * n] += 0.75 * one
                    out[c, 2 * n + 1] += 0.75 * one
                    before = jnp.where(n > 0, 0.25, 0.0)
                    after = jnp.where(2 * n + 2 < run, 0.25, 0.0)
                    out[c, jnp.maximum(2 * n - 1, 0)] += before * one
                    out[c, jnp.minimum(2 * n + 2, depth - 1)] += after * one
                return 0

            lax.fori_loop(0, 3, component, 0)

    if ends:
        even = lax.rem(lax.axis_index("slab"), 2) == 0
        for rim, above in zip(rims, (even, jnp.logical_not(even))):
            row = jnp.where(above, run - 1, 0)
            for c in range(3):
                out[c, row] += rim[c]


def permute_up(values):
    slabs = lax.axis_size("slab")
    return lax.ppermute(values, "slab", [(i, i + 1) for i in range(slabs - 1)])


def exchange(one, two):
    slabs = lax.axis_size("slab")
    pairs = [(i, i + 1) for i in range(1, slabs - 1, 2)]
    other = lax.ppermute(two, "slab", pairs + [(j, i) for i, j in pairs])
    return along(one, "slab", 1), other


def along(values, axis, step):
    peers = lax.axis_size(axis)
    return lax.ppermute(values, axis, [(i, i ^ step) for i in range(peers)])


def slab_sums(sums):
    slabs = lax.axis_size("slab")
    step = 1
    while 2 * step < slabs:
        sums = sums + along(sums, "slab", step)
        step *= 2
    return sums, along(sums, "slab", step)


def gather(slots):
    groups = lax.axis_size("grp")
    if groups != 4:
        return [[along(slot, "grp", step) for slot in slots] for step in range(1, groups)]
    by_x, by_y, by_both = {}, {}, {}
    for i in range(0, len(slots), 2):
        j = i + 1
        by_x[i], by_y[j] = along(slots[i], "grp", 1), along(slots[j], "grp", 2)
        by_x[j], by_y[i] = along(slots[j], "grp", 1), along(slots[i], "grp", 2)
        by_both[i], by_both[j] = along(by_x[i], "grp", 2), along(by_y[j], "grp", 1)
    return [[group[i] for i in range(len(slots))] for group in (by_x, by_y, by_both)]


def call(kernel, outs, specs_in, specs_out, scratch=(), cost=None, limit=VMEM_LIMIT, **more):
    return pl.pallas_call(
        kernel,
        out_shape=outs,
        in_specs=specs_in,
        out_specs=specs_out,
        scratch_shapes=list(scratch),
        cost_estimate=cost,
        compiler_params=pltpu.CompilerParams(vmem_limit_bytes=limit),
        **more,
    )


def per_device(forcing, stiffness, anisotropy, coupling, levels, neighbours):
    _, _, depth, height, width = forcing.shape
    slabs = lax.axis_size("slab")
    f, k = forcing[0], stiffness[0]
    levels = levels.T
    an = jnp.transpose(anisotropy, (1, 0, 2))
    cp = jnp.transpose(coupling, (1, 0, 2))
    plane = 4 * height * width
    padded = height + 2 * PAD
    rows3 = shape_of(3, height, width)
    whole = shape_of(3, depth, height, width)

    one, two = call(
        rims_kernel,
        [shape_of(7, height, width)] * 2,
        [SMEM_SPEC, HBM_SPEC, HBM_SPEC],
        [VMEM_SPEC] * 2,
        [pltpu.SemaphoreType.DMA((6,))],
        estimate(0, 28 * plane),
        limit=60 * 1024 * 1024,
        name="rims",
    )(levels, f, k)
    one, two = exchange(one, two)

    zs, w, wl, w0, gx, gys, gz, gl, dots = call(
        functools.partial(first_kernel, slabs),
        [
            shape_of(3, depth + 2, padded, width),
            shape_of(3, depth, height + PAD, width),
            rows3,
            rows3,
            shape_of(depth, height, width),
            shape_of(depth, height + PAD, width),
            shape_of(depth, height, width),
            shape_of(height, width),
            shape_of(8, width),
        ],
        [SMEM_SPEC] * 3 + [VMEM_SPEC] * 4,
        [VMEM_SPEC] * 9,
        [
            pltpu.VMEM((3, depth, height, width), f32),
            pltpu.VMEM((depth + 2, padded, width), f32),
            pltpu.VMEM((depth + 4, height, width), f32),
        ],
        estimate(150 * depth * plane, 150 * plane),
        name="first",
    )(levels, an, cp, f, k, one, two)
    wlo = permute_up(wl)
    part = call(
        functools.partial(second_kernel, slabs),
        shape_of(8, width),
        [SMEM_SPEC] * 3 + [VMEM_SPEC] * 4,
        VMEM_SPEC,
        cost=estimate(30 * depth * plane, 50 * plane),
        name="second",
    )(levels, an, cp, w, gx, gys, gz)
    dots = call(
        functools.partial(cross_kernel, slabs, depth),
        shape_of(8, width),
        [SMEM_SPEC] * 2 + [VMEM_SPEC] * 5,
        VMEM_SPEC,
        cost=estimate(8 * plane, 6 * plane),
        name="cross",
    )(levels, an, w0, gl, wlo, part, dots)
    mine, theirs = slab_sums(dots)
    half = depth // 2
    u, *slots = call(
        solution_kernel,
        [whole] + [rows3] * half,
        [SMEM_SPEC] + [VMEM_SPEC] * 4,
        [VMEM_SPEC] * (1 + half),
        cost=estimate(4 * depth * plane, 90 * plane),
        name="solve",
    )(levels, mine, theirs, zs, w)
    received = gather(slots)
    steps = range(1, len(received) + 1)
    others = [functools.partial(lambda step, g: g ^ step, step) for step in steps]
    early = [slot for group in received for slot in group[:2]]
    edge_one, edge_two = call(
        functools.partial(edges_kernel, others),
        [rows3] * 2,
        [SMEM_SPEC] * 2 + [VMEM_SPEC] * len(early),
        [VMEM_SPEC] * 2,
        [pltpu.VMEM((width, width), jnp.bfloat16)],
        estimate(100 * plane, 40 * plane),
        name="edges",
    )(levels, neighbours, *early)
    rims = exchange(edge_one, edge_two)

    def mix(start, members, which, ends, name):
        pieces = [received[i][j] for i in members for j in which]
        given = pieces + (list(rims) if ends else [])
        return call(
            functools.partial(mix_kernel, [others[i] for i in members], which, depth, ends),
            whole,
            [SMEM_SPEC] * 2 + [VMEM_SPEC] * (1 + len(given)),
            VMEM_SPEC,
            [pltpu.VMEM((width, 2 * width), jnp.bfloat16)],
            estimate(1000 * plane, (48 + 3 * len(given)) * plane),
            input_output_aliases={} if ends else {2: 0},
            name=name,
        )(levels, neighbours, start, *given)

    members = list(range(len(received)))
    mixed = mix(u, members, range(2), False, "mix_one")
    mixed = mix(mixed, members[:-1], range(2, half), False, "mix_two")
    mixed = mix(mixed, members[-1:], range(2, half), True, "mix_three")
    return mixed[None]


def solution(mesh):
    return jax.shard_map(
        per_device,
        mesh=mesh,
        in_specs=(
            P("grp", None, "slab", None, None),
            P("grp", None, "slab", None, None),
            P("grp", None, None),
            P("grp", None, None),
            P(),
            P(),
        ),
        out_specs=P("grp", None, "slab", None, None),
        check_vma=False,
    )
```

```python
import functools

import jax
import jax.numpy as jnp
from jax import lax
from jax.experimental import pallas as pl
from jax.experimental.pallas import tpu as pltpu
from jax.sharding import PartitionSpec as P

CHUNK = 32
PAD = 8
VMEM_SPEC = pl.BlockSpec(memory_space=pltpu.VMEM)
SMEM_SPEC = pl.BlockSpec(memory_space=pltpu.SMEM)
HBM_SPEC = pl.BlockSpec(memory_space=pltpu.HBM)
VMEM_LIMIT = 18 * 1024 * 1024
f32 = jnp.float32


def shape_of(*dims):
    return jax.ShapeDtypeStruct(dims, f32)


def estimate(flops, nbytes):
    return pl.CostEstimate(flops=int(flops), bytes_accessed=int(nbytes), transcendentals=0)


def cells(full, level):
    return lax.shift_right_logical(jnp.int32(full), 2 - level)


def lanes(rows, width):
    return lax.broadcasted_iota(jnp.int32, (rows, width), 1)


def coefficients(an, nx, nz, height):
    wx = nx.astype(f32) / height
    wz = nz.astype(f32) / height
    wx, wz = wx * wx, wz * wz
    return [[an[c, 0, 0] * wx, an[c, 0, 1], an[c, 0, 2] * wz] for c in range(3)]


def fold(values):
    rows = values.shape[0]
    total = values[0:8]
    for start in range(8, rows, 8):
        total = total + values[start : start + 8]
    return total


def rims_kernel(lev, nb, f_hbm, k_hbm, one, two, choice, sems):
    depth = f_hbm.shape[1]
    a = cells(depth, lev[1, lax.axis_index("grp")])
    even = lax.rem(lax.axis_index("slab"), 2) == 0
    started = []
    for i, (rows, last) in enumerate(((one, even), (two, jnp.logical_not(even)))):
        near = jnp.where(last, a - 1, 0)
        far = jnp.where(last, a - 2, 1)
        for j, (source, target) in enumerate(
            (
                (f_hbm.at[:, near], rows.at[0:3]),
                (k_hbm.at[:, near], rows.at[3:6]),
                (k_hbm.at[2, far], rows.at[6]),
            )
        ):
            started.append(pltpu.make_async_copy(source, target, sems.at[3 * i + j]))
    for copy in started:
        copy.start()
    bits = jnp.int32(0)
    for g in range(nb.shape[0]):
        for entry in range(3):
            step = nb[g, entry] ^ g
            bit = lax.shift_left(jnp.int32(1), jnp.clip(step - 1, 0, 30))
            bits = bits | jnp.where((nb[g, entry] >= 0) & (step > 0), bit, 0)
    choice[0] = bits
    for copy in started:
        copy.wait()


def first_kernel(
    slabs, lev, an, cp, f, k, one, two, zs, w, wl, w0, gx, gys, gz, gl, dots, rj, kys, kzs
):
    _, depth, height, width = f.shape
    g = lax.axis_index("grp")
    nx = cells(width, lev[0, g])
    a = cells(depth, lev[1, g])
    co = coefficients(an, nx, a * slabs, height)
    lane = lanes(CHUNK, width)
    in_x = lane < nx
    in_xp = lane < nx - 1
    in_xm = lane > 0
    chunks = range(0, height, CHUNK)
    zero_pad = jnp.zeros((PAD, width), f32)

    def keep(values):
        return jnp.where(in_x, values, 0.0)

    def pad_row(row):
        kys[row, 0:PAD] = zero_pad
        kys[row, height + PAD :] = zero_pad
        for c in range(3):
            zs[c, row, 0:PAD] = zero_pad
            zs[c, row, height + PAD :] = zero_pad

    def stage(row, _):
        pad_row(row + 1)
        for y in chunks:
            kys[row + 1, PAD + y : PAD + y + CHUNK] = keep(k[1, row, y : y + CHUNK])
            kzs[row + 2, y : y + CHUNK] = keep(k[2, row, y : y + CHUNK])
        return 0

    lax.fori_loop(0, a, stage, 0)
    pad_row(0)
    pad_row(a + 1)
    even = lax.rem(lax.axis_index("slab"), 2) == 0
    rims = []
    for rows, above in ((one, even), (two, jnp.logical_not(even))):
        at = jnp.where(above, a + 1, 0)
        near = jnp.where(above, a + 2, 1)
        far = jnp.where(above, a + 3, 0)
        rims.append((rows, at))
        for y in chunks:
            here = slice(y, y + CHUNK)
            kys[at, PAD + y : PAD + y + CHUNK] = keep(rows[4, here])
            kzs[near, here] = keep(rows[5, here])
            kzs[far, here] = keep(rows[6, here])

    def jacobi(f_at, kx_at, row, own):
        for y in chunks:
            kx = keep(kx_at(y))
            kxp = jnp.where(in_xp, pltpu.roll(kx, width - 1, 1), 0.0)
            kxm = jnp.where(in_xm, pltpu.roll(kx, 1, 1), 0.0)
            ky = kys[row, PAD + y : PAD + y + CHUNK]
            kyp = kys[row, PAD + y + 1 : PAD + y + 1 + CHUNK]
            kym = kys[row, PAD + y - 1 : PAD + y - 1 + CHUNK]
            kz = kzs[row + 1, y : y + CHUNK]
            kzp = kzs[row + 2, y : y + CHUNK]
            kzm = kzs[row, y : y + CHUNK]
            sx = kx + 0.5 * (kxp + kxm)
            sy = ky + 0.5 * (kyp + kym)
            sz = kz + 0.5 * (kzp + kzm)
            for c in range(3):
                diagonal = cp[c, 0, c] + co[c][0] * sx + co[c][1] * sy + co[c][2] * sz
                inverse = 1.0 / diagonal
                zs[c, row, PAD + y : PAD + y + CHUNK] = keep(f_at(c, y)) * inverse
                if own:
                    rj[c, row - 1, y : y + CHUNK] = inverse
            if own:
                gx[row - 1, y : y + CHUNK] = jnp.where(in_xp, 0.5 * (kx + kxp), 0.0)
                gys[row - 1, PAD + y : PAD + y + CHUNK] = 0.5 * (ky + kyp)
                gz[row - 1, y : y + CHUNK] = 0.5 * (kz + kzp)

    def own_row(row, _):
        gys[row, 0:PAD] = zero_pad
        jacobi(
            lambda c, y: f[c, row, y : y + CHUNK], lambda y: k[0, row, y : y + CHUNK], row + 1, True
        )
        return 0

    for rows, at in rims:
        jacobi(
            lambda c, y: rows[c, y : y + CHUNK], lambda y: rows[3, y : y + CHUNK], at, False
        )
    lax.fori_loop(0, a, own_row, 0)
    for y in chunks:
        gl[y : y + CHUNK] = 0.5 * (kzs[1, y : y + CHUNK] + kzs[2, y : y + CHUNK])

    def image_row(row, sums):
        s0, s1, s2 = sums
        for c in range(3):
            w[c, row, height:] = zero_pad
        for y in chunks:
            here = slice(y, y + CHUNK)
            mid = slice(PAD + y, PAD + y + CHUNK)
            above = slice(PAD + y + 1, PAD + y + 1 + CHUNK)
            below = slice(PAD + y - 1, PAD + y - 1 + CHUNK)
            fx = gx[row, here]
            fyp, fym = gys[row, mid], gys[row, below]
            fzp = gz[row, here]
            fzm = 0.5 * (kzs[row + 1, here] + kzs[row + 2, here])
            z = [zs[c, row + 1, mid] for c in range(3)]
            for c in range(3):
                tx = fx * pltpu.roll(z[c], width - 1, 1) + pltpu.roll(fx * z[c], 1, 1)
                ty = fyp * zs[c, row + 1, above] + fym * zs[c, row + 1, below]
                tz = fzp * zs[c, row + 2, mid] + fzm * zs[c, row, mid]
                v = co[c][0] * tx + co[c][1] * ty + co[c][2] * tz
                for other in range(3):
                    if other != c:
                        v = v - cp[c, 0, other] * z[other]
                force = keep(f[c, row, here])
                image = force - v
                scaled = z[c] - v * rj[c, row, here]
                w[c, row, here] = scaled
                s0 = s0 + fold(force * z[c])
                s1 = s1 + fold(image * z[c])
                s2 = s2 + fold(image * scaled)
        return s0, s1, s2

    nothing = jnp.zeros((8, width), f32)
    s0, s1, s2 = lax.fori_loop(0, a, image_row, (nothing, nothing, nothing))
    for c in range(3):
        for y in chunks:
            wl[c, y : y + CHUNK] = w[c, a - 1, y : y + CHUNK]
            w0[c, y : y + CHUNK] = w[c, 0, y : y + CHUNK]
    dots[...] = jnp.zeros((8, width), f32)
    for i, total in enumerate((s0, s1, s2)):
        dots[i : i + 1, :] = jnp.sum(total, axis=0, keepdims=True)


def second_kernel(slabs, lev, an, cp, w, gx, gys, gz, part):
    depth, height, width = gx.shape
    g = lax.axis_index("grp")
    nx = cells(width, lev[0, g])
    a = cells(depth, lev[1, g])
    co = coefficients(an, nx, a * slabs, height)

    def row_sum(row, total, inner):
        for y in range(0, height, CHUNK):
            here = slice(y, y + CHUNK)
            fx, fy = gx[row, here], gys[row, PAD + y : PAD + y + CHUNK]
            fz = gz[row, here] if inner else None
            own = [w[c, row, here] for c in range(3)]
            for c in range(3):
                v = co[c][0] * (fx * pltpu.roll(own[c], width - 1, 1))
                v = v + co[c][1] * (fy * w[c, row, y + 1 : y + 1 + CHUNK])
                if inner:
                    v = v + co[c][2] * (fz * w[c, row + 1, here])
                if c < 2:
                    v = v - cp[c, 0, c + 1] * own[c + 1]
                if c == 0:
                    v = v - cp[0, 0, 2] * own[2]
                total = total + fold(v * own[c])
        return total

    total = lax.fori_loop(
        0, a - 1, lambda row, t: row_sum(row, t, True), jnp.zeros((8, width), f32)
    )
    part[...] = 2.0 * row_sum(a - 1, total, False)


def cross_kernel(slabs, depth, lev, an, w0, gl, wlo, part, dots, out):
    height, width = gl.shape
    g = lax.axis_index("grp")
    nx = cells(width, lev[0, g])
    a = cells(depth, lev[1, g])
    co = coefficients(an, nx, a * slabs, height)
    total = jnp.zeros((8, width), f32)
    for y in range(0, height, CHUNK):
        here = slice(y, y + CHUNK)
        v = jnp.zeros((CHUNK, width), f32)
        for c in range(3):
            v = v + co[c][2] * (w0[c, here] * wlo[c, here])
        total = total + fold(gl[here] * v)
    out[...] = dots[...]
    out[3:4, :] = jnp.sum(part[...] + 2.0 * total, axis=0, keepdims=True)


def slot_rows(depth, run):
    half, quarter = depth // 2, depth // 4
    last = jnp.where(run == quarter, quarter - 1, half - 1)
    rest = [n for n in range(1, half - 1) if n != quarter - 1]
    return [0, last] + rest + [half + quarter - 2 - last]


def solution_kernel(lev, mine, theirs, zs, w, u, *slots):
    _, depth, height, width = u.shape
    half = depth // 2
    g = lax.axis_index("grp")
    a = cells(depth, lev[1, g])
    narrow = lev[0, g] < 2
    sums = jnp.sum(mine[...] + theirs[...], axis=1, keepdims=True)
    sums = jnp.broadcast_to(sums, (8, width))
    d0, d1, d2, e3 = sums[0:1], sums[1:2], sums[2:3], sums[3:4]
    d3 = d2 - e3
    first = d0 / d1
    rz = first * first * d2 - d0
    more = 1.0 + rz / d0
    bend = more * more * d1 - 2.0 * first * more * d2 + first * first * d3
    second = rz / bend
    alpha = jnp.broadcast_to(first + second * more, (CHUNK, width))
    beta = jnp.broadcast_to(-second * first, (CHUNK, width))
    chunks = range(0, height, CHUNK)

    def active_row(row, _):
        for c in range(3):
            for y in chunks:
                z = zs[c, row + 1, PAD + y : PAD + y + CHUNK]
                u[c, row, y : y + CHUNK] = alpha * z + beta * w[c, row, y : y + CHUNK]
        return 0

    def idle_row(row, _):
        for c in range(3):
            for y in chunks:
                u[c, row, y : y + CHUNK] = jnp.zeros((CHUNK, width), f32)
        return 0

    lax.fori_loop(0, a, active_row, 0)
    lax.fori_loop(a, depth, idle_row, 0)
    share = jnp.where(narrow, 1.0, 0.0)
    for slot, n in zip(slots, slot_rows(depth, a)):
        for c in range(3):
            for y in chunks:
                here = slice(y, y + CHUNK)
                beside = pltpu.roll(u[c, n + half, here], width // 2, 1)
                slot[c, here] = u[c, n, here] + share * beside


def role(lev, nb, g, p):
    n0, n1, n2 = nb[g, 0], nb[g, 1], nb[g, 2]
    sign = jnp.where(n2 == p, 1.0, 0.0) - jnp.where((n0 == p) | (n1 == p), 1.0, 0.0)
    coarse = lev[1, p] < lev[1, g]
    return sign.astype(f32), coarse


def x_weights(lev, g, p, sign, width):
    to_x = cells(width, lev[0, g])
    from_x = cells(width, lev[0, p])
    source = lax.broadcasted_iota(jnp.int32, (width, 2 * width), 0)
    target = lax.broadcasted_iota(jnp.int32, (width, 2 * width), 1)
    second = target >= width
    target = jnp.where(second, target - width, target)
    shift = jnp.where(second, width // 2, 0)
    cell = source - shift
    ratio = from_x.astype(f32) / to_x.astype(f32)
    along = (target.astype(f32) + 0.5) * ratio
    weight = jnp.maximum(0.0, 1.0 - jnp.abs(along - (cell.astype(f32) + 0.5)))
    fits = (target < to_x) & (cell >= 0) & (cell < from_x)
    fits = fits & (jnp.logical_not(second) | (lev[0, p] < 2))
    return jnp.where(fits, weight * sign, 0.0).astype(jnp.bfloat16)


def split_dot(values, weights):
    high = values.astype(jnp.bfloat16)
    rest = values - high.astype(f32)
    middle = rest.astype(jnp.bfloat16)
    low = (rest - middle.astype(f32)).astype(jnp.bfloat16)
    dot = functools.partial(jnp.dot, preferred_element_type=f32)
    return dot(high, weights) + (dot(middle, weights) + dot(low, weights))


def edges_kernel(others, lev, nb, *refs):
    pieces = refs[: 2 * len(others)]
    one, two, weights = refs[2 * len(others) :]
    width = one.shape[2]
    g = lax.axis_index("grp")
    even = lax.rem(lax.axis_index("slab"), 2) == 0
    one[...] = jnp.zeros(one.shape, f32)
    two[...] = jnp.zeros(two.shape, f32)
    for i, other in enumerate(others):
        first, last = pieces[2 * i : 2 * i + 2]
        p = other(g)
        sign, coarse = role(lev, nb, g, p)

        @pl.when((sign != 0.0) & coarse)
        def _():
            weights[...] = x_weights(lev, g, p, sign, width)[:, :width]

            def component(c, _):
                below = 0.25 * split_dot(first[c], weights[...])
                above = 0.25 * split_dot(last[c], weights[...])
                one[c] += jnp.where(even, above, below)
                two[c] += jnp.where(even, below, above)
                return 0

            lax.fori_loop(0, 3, component, 0)


def mix_kernel(others, which, depth, ends, lev, nb, start, *refs):
    pieces = refs[: len(which) * len(others)]
    rims = refs[len(pieces) : len(pieces) + (2 if ends else 0)]
    out, weights = refs[len(pieces) + len(rims) :]
    width = start.shape[3]
    half = depth // 2
    g = lax.axis_index("grp")
    run = cells(depth, lev[1, g])

    def begin(c, _):
        for row in range(depth):
            out[c, row] = start[c, row]
        return 0

    lax.fori_loop(0, 3, begin, 0)
    for i, other in enumerate(others):
        p = other(g)
        sign, coarse = role(lev, nb, g, p)
        slots = pieces[len(which) * i : len(which) * (i + 1)]
        order = slot_rows(depth, cells(depth, lev[1, p]))
        rows = [order[j] for j in which]

        @pl.when(sign != 0.0)
        def _():
            weights[...] = x_weights(lev, g, p, sign, width)

        @pl.when((sign != 0.0) & jnp.logical_not(coarse))
        def _():
            def component(c, _):
                for n, slot in zip(rows, slots):
                    both = split_dot(slot[c], weights[...])
                    out[c, n] += both[:, :width]
                    out[c, n + half] += both[:, width:]
                return 0

            lax.fori_loop(0, 3, component, 0)

        @pl.when((sign != 0.0) & coarse)
        def _():
            def component(c, _):
                for n, slot in zip(rows, slots):
                    one = split_dot(slot[c], weights[:, :width])
                    out[c, 2 * n] += 0.75 * one
                    out[c, 2 * n + 1] += 0.75 * one
                    before = jnp.where(n > 0, 0.25, 0.0)
                    after = jnp.where(2 * n + 2 < run, 0.25, 0.0)
                    out[c, jnp.maximum(2 * n - 1, 0)] += before * one
                    out[c, jnp.minimum(2 * n + 2, depth - 1)] += after * one
                return 0

            lax.fori_loop(0, 3, component, 0)

    if ends:
        even = lax.rem(lax.axis_index("slab"), 2) == 0
        for rim, above in zip(rims, (even, jnp.logical_not(even))):
            row = jnp.where(above, run - 1, 0)
            for c in range(3):
                out[c, row] += rim[c]


def permute_up(values):
    slabs = lax.axis_size("slab")
    return lax.ppermute(values, "slab", [(i, i + 1) for i in range(slabs - 1)])


def exchange(one, two):
    slabs = lax.axis_size("slab")
    pairs = [(i, i + 1) for i in range(1, slabs - 1, 2)]
    other = lax.ppermute(two, "slab", pairs + [(j, i) for i, j in pairs])
    return along(one, "slab", 1), other


def along(values, axis, step):
    peers = lax.axis_size(axis)
    return lax.ppermute(values, axis, [(i, i ^ step) for i in range(peers)])


def slab_sums(sums):
    slabs = lax.axis_size("slab")
    step = 1
    while 2 * step < slabs:
        sums = sums + along(sums, "slab", step)
        step *= 2
    return sums, along(sums, "slab", step)


def gather(slots, steps):
    got = {step: {} for step in steps}
    if 3 not in steps or len(steps) == 1 or max(steps) > 3:
        for i, slot in enumerate(slots):
            for step in steps:
                got[step][i] = along(slot, "grp", step)
    elif len(steps) == 2:
        direct = steps[0]
        for i, slot in enumerate(slots):
            got[direct][i] = along(slot, "grp", direct)
            got[3][i] = along(got[direct][i], "grp", 3 ^ direct)
    else:
        for i in range(0, len(slots), 2):
            j = i + 1
            got[1][i], got[2][j] = along(slots[i], "grp", 1), along(slots[j], "grp", 2)
            got[1][j], got[2][i] = along(slots[j], "grp", 1), along(slots[i], "grp", 2)
            got[3][i], got[3][j] = along(got[1][i], "grp", 2), along(got[2][j], "grp", 1)
    return [[got[step][i] for i in range(len(slots))] for step in steps]


def call(kernel, outs, specs_in, specs_out, scratch=(), cost=None, limit=VMEM_LIMIT, **more):
    return pl.pallas_call(
        kernel,
        out_shape=outs,
        in_specs=specs_in,
        out_specs=specs_out,
        scratch_shapes=list(scratch),
        cost_estimate=cost,
        compiler_params=pltpu.CompilerParams(vmem_limit_bytes=limit),
        **more,
    )


def difference(depth, height, width, steps, levels, neighbours, u, *slots):
    half = depth // 2
    plane = 4 * height * width
    rows3 = shape_of(3, height, width)
    whole = shape_of(3, depth, height, width)
    received = gather(slots, steps) if steps else []
    others = [functools.partial(lambda step, g: g ^ step, step) for step in steps]
    early = [slot for group in received for slot in group[:2]]
    if not steps:
        return call(
            functools.partial(mix_kernel, [], [], depth, False),
            whole,
            [SMEM_SPEC] * 2 + [VMEM_SPEC],
            VMEM_SPEC,
            [pltpu.VMEM((width, 2 * width), jnp.bfloat16)],
            name="mix_none",
        )(levels, neighbours, u)
    edge_one, edge_two = call(
        functools.partial(edges_kernel, others),
        [rows3] * 2,
        [SMEM_SPEC] * 2 + [VMEM_SPEC] * len(early),
        [VMEM_SPEC] * 2,
        [pltpu.VMEM((width, width), jnp.bfloat16)],
        estimate(100 * plane, 40 * plane),
        name="edges",
    )(levels, neighbours, *early)
    rims = exchange(edge_one, edge_two)

    def mix(start, members, which, ends, name):
        pieces = [received[i][j] for i in members for j in which]
        given = pieces + (list(rims) if ends else [])
        return call(
            functools.partial(mix_kernel, [others[i] for i in members], which, depth, ends),
            whole,
            [SMEM_SPEC] * 2 + [VMEM_SPEC] * (1 + len(given)),
            VMEM_SPEC,
            [pltpu.VMEM((width, 2 * width), jnp.bfloat16)],
            estimate(1000 * plane, (48 + 3 * len(given)) * plane),
            input_output_aliases={} if ends else {2: 0},
            name=name,
        )(levels, neighbours, start, *given)

    members = list(range(len(received)))
    mixed = mix(u, members, range(2), False, "mix_one")
    if len(steps) == 3:
        mixed = mix(mixed, members[:-1], range(2, half), False, "mix_two")
        return mix(mixed, members[-1:], range(2, half), True, "mix_three")
    mixed = mix(mixed, members, range(2, half - 1), False, "mix_two")
    return mix(mixed, members, range(half - 1, half), True, "mix_three")


def per_device(forcing, stiffness, anisotropy, coupling, levels, neighbours):
    _, _, depth, height, width = forcing.shape
    slabs = lax.axis_size("slab")
    f, k = forcing[0], stiffness[0]
    levels = levels.T
    an = jnp.transpose(anisotropy, (1, 0, 2))
    cp = jnp.transpose(coupling, (1, 0, 2))
    plane = 4 * height * width
    padded = height + 2 * PAD
    rows3 = shape_of(3, height, width)
    whole = shape_of(3, depth, height, width)

    one, two, choice = call(
        rims_kernel,
        [shape_of(7, height, width)] * 2 + [jax.ShapeDtypeStruct((1,), jnp.int32)],
        [SMEM_SPEC, SMEM_SPEC, HBM_SPEC, HBM_SPEC],
        [VMEM_SPEC] * 2 + [SMEM_SPEC],
        [pltpu.SemaphoreType.DMA((6,))],
        estimate(0, 28 * plane),
        limit=60 * 1024 * 1024,
        name="rims",
    )(levels, neighbours, f, k)
    one, two = exchange(one, two)

    zs, w, wl, w0, gx, gys, gz, gl, dots = call(
        functools.partial(first_kernel, slabs),
        [
            shape_of(3, depth + 2, padded, width),
            shape_of(3, depth, height + PAD, width),
            rows3,
            rows3,
            shape_of(depth, height, width),
            shape_of(depth, height + PAD, width),
            shape_of(depth, height, width),
            shape_of(height, width),
            shape_of(8, width),
        ],
        [SMEM_SPEC] * 3 + [VMEM_SPEC] * 4,
        [VMEM_SPEC] * 9,
        [
            pltpu.VMEM((3, depth, height, width), f32),
            pltpu.VMEM((depth + 2, padded, width), f32),
            pltpu.VMEM((depth + 4, height, width), f32),
        ],
        estimate(150 * depth * plane, 150 * plane),
        name="first",
    )(levels, an, cp, f, k, one, two)
    wlo = permute_up(wl)
    part = call(
        functools.partial(second_kernel, slabs),
        shape_of(8, width),
        [SMEM_SPEC] * 3 + [VMEM_SPEC] * 4,
        VMEM_SPEC,
        cost=estimate(30 * depth * plane, 50 * plane),
        name="second",
    )(levels, an, cp, w, gx, gys, gz)
    dots = call(
        functools.partial(cross_kernel, slabs, depth),
        shape_of(8, width),
        [SMEM_SPEC] * 2 + [VMEM_SPEC] * 5,
        VMEM_SPEC,
        cost=estimate(8 * plane, 6 * plane),
        name="cross",
    )(levels, an, w0, gl, wlo, part, dots)
    mine, theirs = slab_sums(dots)
    half = depth // 2
    u, *slots = call(
        solution_kernel,
        [whole] + [rows3] * half,
        [SMEM_SPEC] + [VMEM_SPEC] * 4,
        [VMEM_SPEC] * (1 + half),
        cost=estimate(4 * depth * plane, 90 * plane),
        name="solve",
    )(levels, mine, theirs, zs, w)
    combine = functools.partial(difference, depth, height, width)
    groups = lax.axis_size("grp")
    if groups != 4:
        return combine(tuple(range(1, groups)), levels, neighbours, u, *slots)[None]
    branches = [
        functools.partial(combine, tuple(s for i, s in enumerate((1, 2, 3)) if mask >> i & 1))
        for mask in range(8)
    ]
    return lax.switch(choice[0], branches, levels, neighbours, u, *slots)[None]


def solution(mesh):
    return jax.shard_map(
        per_device,
        mesh=mesh,
        in_specs=(
            P("grp", None, "slab", None, None),
            P("grp", None, "slab", None, None),
            P("grp", None, None),
            P("grp", None, None),
            P(),
            P(),
        ),
        out_specs=P("grp", None, "slab", None, None),
        check_vma=False,
    )
```

```python
import functools

import jax
import jax.numpy as jnp
from jax import lax
from jax.experimental import pallas as pl
from jax.experimental.pallas import tpu as pltpu
from jax.sharding import PartitionSpec as P

CHUNK = 32
PAD = 8
VMEM_SPEC = pl.BlockSpec(memory_space=pltpu.VMEM)
SMEM_SPEC = pl.BlockSpec(memory_space=pltpu.SMEM)
HBM_SPEC = pl.BlockSpec(memory_space=pltpu.HBM)
VMEM_LIMIT = 18 * 1024 * 1024
f32 = jnp.float32


def shape_of(*dims):
    return jax.ShapeDtypeStruct(dims, f32)


def estimate(flops, nbytes):
    return pl.CostEstimate(flops=int(flops), bytes_accessed=int(nbytes), transcendentals=0)


def cells(full, level):
    return lax.shift_right_logical(jnp.int32(full), 2 - level)


def lanes(rows, width):
    return lax.broadcasted_iota(jnp.int32, (rows, width), 1)


def coefficients(an, nx, nz, height):
    wx = nx.astype(f32) / height
    wz = nz.astype(f32) / height
    wx, wz = wx * wx, wz * wz
    return [[an[c, 0, 0] * wx, an[c, 0, 1], an[c, 0, 2] * wz] for c in range(3)]


def fold(values):
    rows = values.shape[0]
    total = values[0:8]
    for start in range(8, rows, 8):
        total = total + values[start : start + 8]
    return total


def rims_kernel(lev, nb, f_hbm, k_hbm, one, two, choice, sems):
    depth = f_hbm.shape[1]
    a = cells(depth, lev[1, lax.axis_index("grp")])
    even = lax.rem(lax.axis_index("slab"), 2) == 0
    started = []
    for i, (rows, last) in enumerate(((one, even), (two, jnp.logical_not(even)))):
        near = jnp.where(last, a - 1, 0)
        far = jnp.where(last, a - 2, 1)
        for j, (source, target) in enumerate(
            (
                (f_hbm.at[:, near], rows.at[0:3]),
                (k_hbm.at[:, near], rows.at[3:6]),
                (k_hbm.at[2, far], rows.at[6]),
            )
        ):
            started.append(pltpu.make_async_copy(source, target, sems.at[3 * i + j]))
    for copy in started:
        copy.start()
    bits = jnp.int32(0)
    for g in range(nb.shape[0]):
        for entry in range(3):
            step = nb[g, entry] ^ g
            bit = lax.shift_left(jnp.int32(1), jnp.clip(step - 1, 0, 30))
            bits = bits | jnp.where((nb[g, entry] >= 0) & (step > 0), bit, 0)
    choice[0] = bits
    for copy in started:
        copy.wait()


def jacobi(height, masks, cp, co, f_at, kx_at, ky_at, kz_at, z_to, inverse_to=None, faces_to=None):
    in_x, in_xp, in_xm = masks
    for y in range(0, height, CHUNK):
        kx = kx_at(y)
        kxp = jnp.where(in_xp, pltpu.roll(kx, kx.shape[1] - 1, 1), 0.0)
        kxm = jnp.where(in_xm, pltpu.roll(kx, 1, 1), 0.0)
        ky, kyp, kym = ky_at(y, 0), ky_at(y, 1), ky_at(y, -1)
        kz, kzp, kzm = kz_at(y, 0), kz_at(y, 1), kz_at(y, -1)
        sx = kx + 0.5 * (kxp + kxm)
        sy = ky + 0.5 * (kyp + kym)
        sz = kz + 0.5 * (kzp + kzm)
        for c in range(3):
            diagonal = cp[c, 0, c] + co[c][0] * sx + co[c][1] * sy + co[c][2] * sz
            inverse = 1.0 / diagonal
            z_to(c, y, f_at(c, y) * inverse)
            if inverse_to is not None:
                inverse_to(c, y, inverse)
        if faces_to is not None:
            faces_to(y, jnp.where(in_xp, 0.5 * (kx + kxp), 0.0), 0.5 * (ky + kyp), 0.5 * (kz + kzp))


def image(c, cp, co, fx, fyp, fym, fzp, fzm, z, above, below, up, down):
    width = fx.shape[1]
    tx = fx * pltpu.roll(z[c], width - 1, 1) + pltpu.roll(fx * z[c], 1, 1)
    v = co[c][0] * tx + co[c][1] * (fyp * above + fym * below) + co[c][2] * (fzp * up + fzm * down)
    for other in range(3):
        if other != c:
            v = v - cp[c, 0, other] * z[other]
    return v


def settings(slabs, lev, an, depth, height, width):
    g = lax.axis_index("grp")
    nx = cells(width, lev[0, g])
    a = cells(depth, lev[1, g])
    lane = lanes(CHUNK, width)
    masks = (lane < nx, lane < nx - 1, lane > 0)
    return a, coefficients(an, nx, a * slabs, height), masks


def own_kernel(slabs, lev, an, cp, f, k, zs, rj, gx, gys, gz, kys):
    _, depth, height, width = f.shape
    a, co, masks = settings(slabs, lev, an, depth, height, width)
    zero_pad = jnp.zeros((PAD, width), f32)

    def keep(values):
        return jnp.where(masks[0], values, 0.0)

    def own_row(row, _):
        kys[row, 0:PAD] = zero_pad
        kys[row, height + PAD :] = zero_pad
        gys[row, 0:PAD] = zero_pad
        for c in range(3):
            zs[c, row, 0:PAD] = zero_pad
            zs[c, row, height + PAD :] = zero_pad
        for y in range(0, height, CHUNK):
            kys[row, PAD + y : PAD + y + CHUNK] = keep(k[1, row, y : y + CHUNK])

        def beside(step):
            return jnp.clip(row + step, 0, depth - 1)

        def z_to(c, y, value):
            zs[c, row, PAD + y : PAD + y + CHUNK] = value

        def inverse_to(c, y, value):
            rj[c, row, y : y + CHUNK] = value

        def faces_to(y, fx, fy, fz):
            gx[row, y : y + CHUNK] = fx
            gys[row, PAD + y : PAD + y + CHUNK] = fy
            gz[row, y : y + CHUNK] = fz

        jacobi(
            height,
            masks,
            cp,
            co,
            lambda c, y: keep(f[c, row, y : y + CHUNK]),
            lambda y: keep(k[0, row, y : y + CHUNK]),
            lambda y, step: kys[row, PAD + y + step : PAD + y + step + CHUNK],
            lambda y, step: keep(k[2, beside(step), y : y + CHUNK]),
            z_to,
            inverse_to,
            faces_to,
        )
        return 0

    lax.fori_loop(0, a, own_row, 0)


def edge_kernel(slabs, lev, an, cp, f, k, one, two, zs, gx, gys, gz, kys, zb, rb, gb, wl, kyr):
    _, depth, height, width = f.shape
    a, co, masks = settings(slabs, lev, an, depth, height, width)
    zero_pad = jnp.zeros((PAD, width), f32)
    even = lax.rem(lax.axis_index("slab"), 2) == 0
    last = a - 1
    chunks = range(0, height, CHUNK)

    def keep(values):
        return jnp.where(masks[0], values, 0.0)

    for row in range(2):
        kyr[row, 0:PAD] = zero_pad
        kyr[row, height + PAD :] = zero_pad
    for row in range(4):
        for c in range(3):
            zb[c, row, 0:PAD] = zero_pad
            zb[c, row, height + PAD :] = zero_pad

    def rim(rows, above, own, slot):
        def own_kz(y):
            return keep(k[2, own, y : y + CHUNK])

        for y in chunks:
            here = slice(y, y + CHUNK)
            kyr[slot, PAD + y : PAD + y + CHUNK] = keep(rows[4, here])
            gb[above, here] = 0.5 * (own_kz(y) + keep(rows[5, here]))

        def z_to(c, y, value):
            zb[c, 3 * above, PAD + y : PAD + y + CHUNK] = value

        jacobi(
            height,
            masks,
            cp,
            co,
            lambda c, y: keep(rows[c, y : y + CHUNK]),
            lambda y: keep(rows[3, y : y + CHUNK]),
            lambda y, step: kyr[slot, PAD + y + step : PAD + y + step + CHUNK],
            lambda y, step: own_kz(y) if step < 0 else keep(rows[5 + step, y : y + CHUNK]),
            z_to,
        )

        def own_z_to(c, y, value):
            zb[c, 1 + above, PAD + y : PAD + y + CHUNK] = value

        def inverse_to(c, y, value):
            rb[c, above, y : y + CHUNK] = value

        inner = jnp.where(above == 1, a - 2, 1)

        def kz_at(y, step):
            if step == 0:
                return own_kz(y)
            if step > 0:
                return keep(rows[5, y : y + CHUNK])
            return keep(k[2, inner, y : y + CHUNK])

        jacobi(
            height,
            masks,
            cp,
            co,
            lambda c, y: keep(f[c, own, y : y + CHUNK]),
            lambda y: keep(k[0, own, y : y + CHUNK]),
            lambda y, step: kys[own, PAD + y + step : PAD + y + step + CHUNK],
            kz_at,
            own_z_to,
            inverse_to,
        )

    for slot, (rows, is_above) in enumerate(((one, even), (two, jnp.logical_not(even)))):
        rim(rows, is_above.astype(jnp.int32), jnp.where(is_above, last, 0), slot)

    short = a == 2
    for y in chunks:
        here = slice(y, y + CHUNK)
        mid = slice(PAD + y, PAD + y + CHUNK)
        fzm = gz[a - 2, here]
        z = [zb[c, 2, mid] for c in range(3)]
        for c in range(3):
            v = image(
                c,
                cp,
                co,
                gx[last, here],
                gys[last, mid],
                gys[last, PAD + y - 1 : PAD + y - 1 + CHUNK],
                gb[1, here],
                fzm,
                z,
                zb[c, 2, PAD + y + 1 : PAD + y + 1 + CHUNK],
                zb[c, 2, PAD + y - 1 : PAD + y - 1 + CHUNK],
                zb[c, 3, mid],
                jnp.where(short, zb[c, 1, mid], zs[c, a - 2, mid]),
            )
            wl[c, here] = z[c] - v * rb[c, 1, here]


def image_kernel(
    slabs, lev, an, cp, f, zs, zb, rj, rb, gx, gys, gz, gb, zf, w, w0, dots, rf, gf
):
    _, depth, height, width = f.shape
    a, co, masks = settings(slabs, lev, an, depth, height, width)
    chunks = range(0, height, CHUNK)
    pads = height + 2 * PAD

    def copy_row(row, _):
        for c in range(3):
            for y in range(0, pads, PAD):
                zf[c, row + 1, y : y + PAD] = zs[c, row, y : y + PAD]
            for y in chunks:
                rf[c, row, y : y + CHUNK] = rj[c, row, y : y + CHUNK]
        for y in chunks:
            gf[row + 1, y : y + CHUNK] = gz[row, y : y + CHUNK]
        return 0

    lax.fori_loop(1, a - 1, copy_row, 0)
    for y in chunks:
        gf[1, y : y + CHUNK] = gz[0, y : y + CHUNK]
        gf[0, y : y + CHUNK] = gb[0, y : y + CHUNK]
    for y in chunks:
        gf[a, y : y + CHUNK] = gb[1, y : y + CHUNK]
    for given, row in ((0, 0), (1, 1), (2, a), (3, a + 1)):
        for c in range(3):
            for y in range(0, pads, PAD):
                zf[c, row, y : y + PAD] = zb[c, given, y : y + PAD]
    for given, row in ((0, 0), (1, a - 1)):
        for c in range(3):
            for y in chunks:
                rf[c, row, y : y + CHUNK] = rb[c, given, y : y + CHUNK]

    def image_row(row, sums):
        s0, s1, s2 = sums
        for c in range(3):
            w[c, row, height:] = jnp.zeros((PAD, width), f32)
        for y in chunks:
            here = slice(y, y + CHUNK)
            mid = slice(PAD + y, PAD + y + CHUNK)
            above = slice(PAD + y + 1, PAD + y + 1 + CHUNK)
            below = slice(PAD + y - 1, PAD + y - 1 + CHUNK)
            z = [zf[c, row + 1, mid] for c in range(3)]
            for c in range(3):
                v = image(
                    c,
                    cp,
                    co,
                    gx[row, here],
                    gys[row, mid],
                    gys[row, below],
                    gf[row + 1, here],
                    gf[row, here],
                    z,
                    zf[c, row + 1, above],
                    zf[c, row + 1, below],
                    zf[c, row + 2, mid],
                    zf[c, row, mid],
                )
                force = jnp.where(masks[0], f[c, row, here], 0.0)
                imaged = force - v
                scaled = z[c] - v * rf[c, row, here]
                w[c, row, here] = scaled
                s0 = s0 + fold(force * z[c])
                s1 = s1 + fold(imaged * z[c])
                s2 = s2 + fold(imaged * scaled)
        return s0, s1, s2

    nothing = jnp.zeros((8, width), f32)
    s0, s1, s2 = lax.fori_loop(0, a, image_row, (nothing, nothing, nothing))

    def row_sum(row, total, inner):
        for y in chunks:
            here = slice(y, y + CHUNK)
            fx, fy = gx[row, here], gys[row, PAD + y : PAD + y + CHUNK]
            own = [w[c, row, here] for c in range(3)]
            for c in range(3):
                v = co[c][0] * (fx * pltpu.roll(own[c], width - 1, 1))
                v = v + co[c][1] * (fy * w[c, row, y + 1 : y + 1 + CHUNK])
                if inner:
                    v = v + co[c][2] * (gz[row, here] * w[c, row + 1, here])
                if c < 2:
                    v = v - cp[c, 0, c + 1] * own[c + 1]
                if c == 0:
                    v = v - cp[0, 0, 2] * own[2]
                total = total + fold(v * own[c])
        return total

    s3 = lax.fori_loop(0, a - 1, lambda row, t: row_sum(row, t, True), nothing)
    s3 = 2.0 * row_sum(a - 1, s3, False)
    for c in range(3):
        for y in chunks:
            w0[c, y : y + CHUNK] = w[c, 0, y : y + CHUNK]
    dots[...] = jnp.zeros((8, width), f32)
    for i, total in enumerate((s0, s1, s2, s3)):
        dots[i : i + 1, :] = jnp.sum(total, axis=0, keepdims=True)


def cross_kernel(slabs, depth, lev, an, w0, gb, wlo, dots, out):
    _, height, width = gb.shape
    g = lax.axis_index("grp")
    nx = cells(width, lev[0, g])
    a = cells(depth, lev[1, g])
    co = coefficients(an, nx, a * slabs, height)
    total = jnp.zeros((8, width), f32)
    for y in range(0, height, CHUNK):
        here = slice(y, y + CHUNK)
        v = jnp.zeros((CHUNK, width), f32)
        for c in range(3):
            v = v + co[c][2] * (w0[c, here] * wlo[c, here])
        total = total + fold(gb[0, here] * v)
    out[...] = dots[...]
    out[3:4, :] = dots[3:4, :] + 2.0 * jnp.sum(total, axis=0, keepdims=True)


def slot_rows(depth, run):
    half, quarter = depth // 2, depth // 4
    last = jnp.where(run == quarter, quarter - 1, half - 1)
    rest = [n for n in range(1, half - 1) if n != quarter - 1]
    return [0, last] + rest + [half + quarter - 2 - last]


def solution_kernel(lev, mine, theirs, zs, w, u, *slots):
    _, depth, height, width = u.shape
    half = depth // 2
    g = lax.axis_index("grp")
    a = cells(depth, lev[1, g])
    narrow = lev[0, g] < 2
    sums = jnp.sum(mine[...] + theirs[...], axis=1, keepdims=True)
    sums = jnp.broadcast_to(sums, (8, width))
    d0, d1, d2, e3 = sums[0:1], sums[1:2], sums[2:3], sums[3:4]
    d3 = d2 - e3
    first = d0 / d1
    rz = first * first * d2 - d0
    more = 1.0 + rz / d0
    bend = more * more * d1 - 2.0 * first * more * d2 + first * first * d3
    second = rz / bend
    alpha = jnp.broadcast_to(first + second * more, (CHUNK, width))
    beta = jnp.broadcast_to(-second * first, (CHUNK, width))
    chunks = range(0, height, CHUNK)

    def active_row(row, _):
        for c in range(3):
            for y in chunks:
                z = zs[c, row + 1, PAD + y : PAD + y + CHUNK]
                u[c, row, y : y + CHUNK] = alpha * z + beta * w[c, row, y : y + CHUNK]
        return 0

    def idle_row(row, _):
        for c in range(3):
            for y in chunks:
                u[c, row, y : y + CHUNK] = jnp.zeros((CHUNK, width), f32)
        return 0

    lax.fori_loop(0, a, active_row, 0)
    lax.fori_loop(a, depth, idle_row, 0)
    share = jnp.where(narrow, 1.0, 0.0)
    for slot, n in zip(slots, slot_rows(depth, a)):
        for c in range(3):
            for y in chunks:
                here = slice(y, y + CHUNK)
                beside = pltpu.roll(u[c, n + half, here], width // 2, 1)
                slot[c, here] = u[c, n, here] + share * beside


def role(lev, nb, g, p):
    n0, n1, n2 = nb[g, 0], nb[g, 1], nb[g, 2]
    sign = jnp.where(n2 == p, 1.0, 0.0) - jnp.where((n0 == p) | (n1 == p), 1.0, 0.0)
    coarse = lev[1, p] < lev[1, g]
    return sign.astype(f32), coarse


def x_weights(lev, g, p, sign, width):
    to_x = cells(width, lev[0, g])
    from_x = cells(width, lev[0, p])
    source = lax.broadcasted_iota(jnp.int32, (width, 2 * width), 0)
    target = lax.broadcasted_iota(jnp.int32, (width, 2 * width), 1)
    second = target >= width
    target = jnp.where(second, target - width, target)
    shift = jnp.where(second, width // 2, 0)
    cell = source - shift
    ratio = from_x.astype(f32) / to_x.astype(f32)
    along = (target.astype(f32) + 0.5) * ratio
    weight = jnp.maximum(0.0, 1.0 - jnp.abs(along - (cell.astype(f32) + 0.5)))
    fits = (target < to_x) & (cell >= 0) & (cell < from_x)
    fits = fits & (jnp.logical_not(second) | (lev[0, p] < 2))
    return jnp.where(fits, weight * sign, 0.0).astype(jnp.bfloat16)


def split_dot(values, weights):
    high = values.astype(jnp.bfloat16)
    rest = values - high.astype(f32)
    middle = rest.astype(jnp.bfloat16)
    low = (rest - middle.astype(f32)).astype(jnp.bfloat16)
    dot = functools.partial(jnp.dot, preferred_element_type=f32)
    return dot(high, weights) + (dot(middle, weights) + dot(low, weights))


def edges_kernel(others, lev, nb, *refs):
    pieces = refs[: 2 * len(others)]
    one, two, weights = refs[2 * len(others) :]
    width = one.shape[2]
    g = lax.axis_index("grp")
    even = lax.rem(lax.axis_index("slab"), 2) == 0
    one[...] = jnp.zeros(one.shape, f32)
    two[...] = jnp.zeros(two.shape, f32)
    for i, other in enumerate(others):
        first, last = pieces[2 * i : 2 * i + 2]
        p = other(g)
        sign, coarse = role(lev, nb, g, p)

        @pl.when((sign != 0.0) & coarse)
        def _():
            weights[...] = x_weights(lev, g, p, sign, width)[:, :width]

            def component(c, _):
                below = 0.25 * split_dot(first[c], weights[...])
                above = 0.25 * split_dot(last[c], weights[...])
                one[c] += jnp.where(even, above, below)
                two[c] += jnp.where(even, below, above)
                return 0

            lax.fori_loop(0, 3, component, 0)


def mix_kernel(others, which, depth, ends, lev, nb, start, *refs):
    pieces = refs[: len(which) * len(others)]
    rims = refs[len(pieces) : len(pieces) + (2 if ends else 0)]
    out, weights = refs[len(pieces) + len(rims) :]
    width = start.shape[3]
    half = depth // 2
    g = lax.axis_index("grp")
    run = cells(depth, lev[1, g])

    def begin(c, _):
        for row in range(depth):
            out[c, row] = start[c, row]
        return 0

    lax.fori_loop(0, 3, begin, 0)
    for i, other in enumerate(others):
        p = other(g)
        sign, coarse = role(lev, nb, g, p)
        slots = pieces[len(which) * i : len(which) * (i + 1)]
        order = slot_rows(depth, cells(depth, lev[1, p]))
        rows = [order[j] for j in which]

        @pl.when(sign != 0.0)
        def _():
            weights[...] = x_weights(lev, g, p, sign, width)

        @pl.when((sign != 0.0) & jnp.logical_not(coarse))
        def _():
            def component(c, _):
                for n, slot in zip(rows, slots):
                    both = split_dot(slot[c], weights[...])
                    out[c, n] += both[:, :width]
                    out[c, n + half] += both[:, width:]
                return 0

            lax.fori_loop(0, 3, component, 0)

        @pl.when((sign != 0.0) & coarse)
        def _():
            def component(c, _):
                for n, slot in zip(rows, slots):
                    one = split_dot(slot[c], weights[:, :width])
                    out[c, 2 * n] += 0.75 * one
                    out[c, 2 * n + 1] += 0.75 * one
                    before = jnp.where(n > 0, 0.25, 0.0)
                    after = jnp.where(2 * n + 2 < run, 0.25, 0.0)
                    out[c, jnp.maximum(2 * n - 1, 0)] += before * one
                    out[c, jnp.minimum(2 * n + 2, depth - 1)] += after * one
                return 0

            lax.fori_loop(0, 3, component, 0)

    if ends:
        even = lax.rem(lax.axis_index("slab"), 2) == 0
        for rim, above in zip(rims, (even, jnp.logical_not(even))):
            row = jnp.where(above, run - 1, 0)
            for c in range(3):
                out[c, row] += rim[c]


def permute_up(values):
    slabs = lax.axis_size("slab")
    return lax.ppermute(values, "slab", [(i, i + 1) for i in range(slabs - 1)])


def exchange(one, two):
    slabs = lax.axis_size("slab")
    pairs = [(i, i + 1) for i in range(1, slabs - 1, 2)]
    other = lax.ppermute(two, "slab", pairs + [(j, i) for i, j in pairs])
    return along(one, "slab", 1), other


def along(values, axis, step):
    peers = lax.axis_size(axis)
    return lax.ppermute(values, axis, [(i, i ^ step) for i in range(peers)])


def slab_sums(sums):
    slabs = lax.axis_size("slab")
    step = 1
    while 2 * step < slabs:
        sums = sums + along(sums, "slab", step)
        step *= 2
    return sums, along(sums, "slab", step)


def gather(slots, steps):
    got = {step: {} for step in steps}
    if 3 not in steps or len(steps) == 1 or max(steps) > 3:
        for i, slot in enumerate(slots):
            for step in steps:
                got[step][i] = along(slot, "grp", step)
    elif len(steps) == 2:
        direct = steps[0]
        for i, slot in enumerate(slots):
            got[direct][i] = along(slot, "grp", direct)
            got[3][i] = along(got[direct][i], "grp", 3 ^ direct)
    else:
        for i in range(0, len(slots), 2):
            j = i + 1
            got[1][i], got[2][j] = along(slots[i], "grp", 1), along(slots[j], "grp", 2)
            got[1][j], got[2][i] = along(slots[j], "grp", 1), along(slots[i], "grp", 2)
            got[3][i], got[3][j] = along(got[1][i], "grp", 2), along(got[2][j], "grp", 1)
    return [[got[step][i] for i in range(len(slots))] for step in steps]


def call(kernel, outs, specs_in, specs_out, scratch=(), cost=None, limit=VMEM_LIMIT, **more):
    return pl.pallas_call(
        kernel,
        out_shape=outs,
        in_specs=specs_in,
        out_specs=specs_out,
        scratch_shapes=list(scratch),
        cost_estimate=cost,
        compiler_params=pltpu.CompilerParams(vmem_limit_bytes=limit),
        **more,
    )


def difference(depth, height, width, steps, levels, neighbours, u, *slots):
    half = depth // 2
    plane = 4 * height * width
    rows3 = shape_of(3, height, width)
    whole = shape_of(3, depth, height, width)
    received = gather(slots, steps) if steps else []
    others = [functools.partial(lambda step, g: g ^ step, step) for step in steps]
    early = [slot for group in received for slot in group[:2]]
    if not steps:
        return call(
            functools.partial(mix_kernel, [], [], depth, False),
            whole,
            [SMEM_SPEC] * 2 + [VMEM_SPEC],
            VMEM_SPEC,
            [pltpu.VMEM((width, 2 * width), jnp.bfloat16)],
            name="mix_none",
        )(levels, neighbours, u)
    edge_one, edge_two = call(
        functools.partial(edges_kernel, others),
        [rows3] * 2,
        [SMEM_SPEC] * 2 + [VMEM_SPEC] * len(early),
        [VMEM_SPEC] * 2,
        [pltpu.VMEM((width, width), jnp.bfloat16)],
        estimate(100 * plane, 40 * plane),
        name="edges",
    )(levels, neighbours, *early)
    rims = exchange(edge_one, edge_two)

    def mix(start, members, which, ends, name):
        pieces = [received[i][j] for i in members for j in which]
        given = pieces + (list(rims) if ends else [])
        return call(
            functools.partial(mix_kernel, [others[i] for i in members], which, depth, ends),
            whole,
            [SMEM_SPEC] * 2 + [VMEM_SPEC] * (1 + len(given)),
            VMEM_SPEC,
            [pltpu.VMEM((width, 2 * width), jnp.bfloat16)],
            estimate(1000 * plane, (48 + 3 * len(given)) * plane),
            input_output_aliases={} if ends else {2: 0},
            name=name,
        )(levels, neighbours, start, *given)

    members = list(range(len(received)))
    mixed = mix(u, members, range(2), False, "mix_one")
    if len(steps) == 3:
        mixed = mix(mixed, members[:-1], range(2, half), False, "mix_two")
        return mix(mixed, members[-1:], range(2, half), True, "mix_three")
    mixed = mix(mixed, members, range(2, half - 1), False, "mix_two")
    return mix(mixed, members, range(half - 1, half), True, "mix_three")


def per_device(forcing, stiffness, anisotropy, coupling, levels, neighbours):
    _, _, depth, height, width = forcing.shape
    slabs = lax.axis_size("slab")
    f, k = forcing[0], stiffness[0]
    levels = levels.T
    an = jnp.transpose(anisotropy, (1, 0, 2))
    cp = jnp.transpose(coupling, (1, 0, 2))
    plane = 4 * height * width
    padded = height + 2 * PAD
    rows3 = shape_of(3, height, width)
    whole = shape_of(3, depth, height, width)

    one, two, choice = call(
        rims_kernel,
        [shape_of(7, height, width)] * 2 + [jax.ShapeDtypeStruct((1,), jnp.int32)],
        [SMEM_SPEC, SMEM_SPEC, HBM_SPEC, HBM_SPEC],
        [VMEM_SPEC] * 2 + [SMEM_SPEC],
        [pltpu.SemaphoreType.DMA((6,))],
        estimate(0, 28 * plane),
        limit=60 * 1024 * 1024,
        name="rims",
    )(levels, neighbours, f, k)
    one, two = exchange(one, two)

    coefs = [levels, an, cp]
    zs, rj, gx, gys, gz, kys = call(
        functools.partial(own_kernel, slabs),
        [
            shape_of(3, depth, padded, width),
            whole,
            shape_of(depth, height, width),
            shape_of(depth, height + PAD, width),
            shape_of(depth, height, width),
            shape_of(depth, padded, width),
        ],
        [SMEM_SPEC] * 3 + [VMEM_SPEC] * 2,
        [VMEM_SPEC] * 6,
        cost=estimate(60 * depth * plane, 120 * plane),
        name="own",
    )(*coefs, f, k)
    zb, rb, gb, wl = call(
        functools.partial(edge_kernel, slabs),
        [
            shape_of(3, 4, padded, width),
            shape_of(3, 2, height, width),
            shape_of(2, height, width),
            rows3,
        ],
        [SMEM_SPEC] * 3 + [VMEM_SPEC] * 9,
        [VMEM_SPEC] * 4,
        [pltpu.VMEM((2, padded, width), f32)],
        estimate(150 * plane, 60 * plane),
        name="edge",
    )(*coefs, f, k, one, two, zs, gx, gys, gz, kys)
    wlo = permute_up(wl)
    zf, w, w0, dots = call(
        functools.partial(image_kernel, slabs),
        [
            shape_of(3, depth + 2, padded, width),
            shape_of(3, depth, height + PAD, width),
            rows3,
            shape_of(8, width),
        ],
        [SMEM_SPEC] * 3 + [VMEM_SPEC] * 9,
        [VMEM_SPEC] * 4,
        [pltpu.VMEM((3, depth, height, width), f32), pltpu.VMEM((depth + 1, height, width), f32)],
        estimate(100 * depth * plane, 150 * plane),
        name="image",
    )(*coefs, f, zs, zb, rj, rb, gx, gys, gz, gb)
    dots = call(
        functools.partial(cross_kernel, slabs, depth),
        shape_of(8, width),
        [SMEM_SPEC] * 2 + [VMEM_SPEC] * 4,
        VMEM_SPEC,
        cost=estimate(8 * plane, 8 * plane),
        name="cross",
    )(levels, an, w0, gb, wlo, dots)
    mine, theirs = slab_sums(dots)
    half = depth // 2
    u, *slots = call(
        solution_kernel,
        [whole] + [rows3] * half,
        [SMEM_SPEC] + [VMEM_SPEC] * 4,
        [VMEM_SPEC] * (1 + half),
        cost=estimate(4 * depth * plane, 90 * plane),
        name="solve",
    )(levels, mine, theirs, zf, w)
    combine = functools.partial(difference, depth, height, width)
    groups = lax.axis_size("grp")
    if groups != 4:
        return combine(tuple(range(1, groups)), levels, neighbours, u, *slots)[None]
    branches = [
        functools.partial(combine, tuple(s for i, s in enumerate((1, 2, 3)) if mask >> i & 1))
        for mask in range(8)
    ]
    return lax.switch(choice[0], branches, levels, neighbours, u, *slots)[None]


def solution(mesh):
    return jax.shard_map(
        per_device,
        mesh=mesh,
        in_specs=(
            P("grp", None, "slab", None, None),
            P("grp", None, "slab", None, None),
            P("grp", None, None),
            P("grp", None, None),
            P(),
            P(),
        ),
        out_specs=P("grp", None, "slab", None, None),
        check_vma=False,
    )
```
